128 devices in a mesh: wind: 8 (over z, y_hi), state: 16 (over x, y_lo, core).
Axes of the slice: x: 4, y: 4 (y_hi: 2, y_lo: 2; y = y_hi * 2 + y_lo), z: 4, core: 2. Of those that a mesh axis runs over, the one named last changes fastest.
Arguments:
- value_next: float32 [128, 16, 256, 256], P('wind', None, 'state'), may hold values from -6 to 6
- density: float32 [128, 16, 256, 256], P('wind', None, 'state'), may hold values from 0.1 to 2
- price: float32 [128, 16], P('wind'), may hold values from -4 to 4
- wind_rate: float32 [128, 16], P('wind'), may hold values from 0.05 to 0.5
- tank_inverse: float32 [256, 256], replicated, may hold values from -0.5 to 1.5
- soc_inverse: float32 [256, 256], replicated, may hold values from -0.5 to 1.5
Outputs:
- value: float32 [128, 16, 256, 256], P('wind', None, 'state')
- density_next: float32 [128, 16, 256, 256], P('wind', None, 'state')
The draws below stay inside these ranges and needn't reach their ends.
All inputs are finite; a program needn't handle non-finite values.
Results may differ from the reference program's by a relative error of at most 0.0001.
Values sent between devices are 32-bit elements; how exact they have to be, the bound alone decides.
A program may use at most 192 MiB of HBM per device.

```python
import math
import jax
import jax.numpy as jnp
from jax import lax

S = 256
K = 256
W = 128
ROOM = 16
ITERS = 4


def implicit_inverse(key, order, spread):
    first, second = jax.random.split(jax.random.fold_in(key, 17))
    diagonal = jax.random.uniform(first, (order,), jnp.float32, 0.8, 1.2)
    offdiag = jax.random.normal(second, (order, order), jnp.float32) * (spread / order ** 0.5)
    offdiag = jnp.clip(offdiag, -0.45, 0.45)
    return jnp.eye(order, dtype=jnp.float32) * diagonal[:, None] + offdiag


def draw_tank_inverse(key, part):
    spread = 0.4
    return implicit_inverse(jax.random.fold_in(key, 3), K, spread)


def draw_soc_inverse(key, part):
    spread = 0.4
    return implicit_inverse(jax.random.fold_in(key, 5), S, spread)


def block_scale(key, shape, cuts, least, top_value):
    factor_of = 1.0
    for position, blocks in cuts:
        steps = jax.random.uniform(jax.random.fold_in(jax.random.fold_in(key, 6), position), (blocks,), jnp.float32, least / len(cuts), top_value / len(cuts))
        factor_of = factor_of * jnp.repeat(jnp.exp(steps), shape[position] // blocks).reshape((-1,) + (1,) * (len(shape) - 1 - position))
    return factor_of


def normal_values(stream_key, extent, deviation, reach, cuts=(), held_as=jnp.bfloat16):
    array = jax.random.normal(stream_key, extent, jnp.float32) * deviation
    if len(cuts) > 0:
        array = block_scale(stream_key, extent, cuts, -0.22, 0.18) * array
    return jnp.clip(array, min=-reach, max=reach).astype(held_as)


def setup_inputs(seed: int = 0) -> dict:
    keys = jax.random.split(jax.random.key(seed), 7)
    return {
        "value_next": normal_values(keys[0], (W, ROOM, S, K), 1.0, 6.0, ((0, 8), (2, 16)), jnp.float32),
        "density": jnp.clip(0.1 + 1.9 * jax.random.uniform(keys[1], (W, ROOM, K, S), jnp.float32) ** block_scale(keys[1], (W, ROOM, K, S), ((0, 8), (2, 16)), -0.2, 0.2), 0.1, 2.0),
        "price": normal_values(keys[2], (W, ROOM), 1.0, 4.0, ((0, 8),), jnp.float32),
        "wind_rate": jnp.clip(jnp.exp(math.log(0.5) - 2.3025851 * jax.random.uniform(keys[3], (W, ROOM), jnp.float32) ** block_scale(keys[3], (W, ROOM), ((0, 8),), -0.2, 0.2)), 0.05, 0.5),
        "tank_inverse": draw_tank_inverse(jax.random.fold_in(keys[6], 71), 0),
        "soc_inverse": draw_soc_inverse(jax.random.fold_in(keys[6], 71), 0),
    }


step_size = 0.25
control_bound = 2.0
control_cost = 1.0
tank_spread = 0.3


def neighbours(field, axis):
    widths = [(0, 0)] * field.ndim
    widths[axis] = (1, 1)
    padded = jnp.pad(field, widths)
    length = field.shape[axis]
    upper = lax.slice_in_dim(padded, 2, length + 2, axis=axis)
    lower = lax.slice_in_dim(padded, 0, length, axis=axis)
    return upper, lower


def control_law(current, price):
    upper, lower = neighbours(current, 2)
    shifted = 0.5 * (upper - lower) + price[:, :, None, None]
    action = -control_bound * jnp.tanh(shifted / (control_cost * control_bound))
    hamilton = action * shifted + 0.5 * control_cost * action * action
    return action, hamilton


def reference(value_next, density, price, wind_rate, tank_inverse, soc_inverse):
    current = value_next
    for sweep in range(ITERS):
        action, hamilton = control_law(current, price)
        upper, lower = neighbours(current, 0)
        couple = wind_rate[:, :, None, None] * (upper + lower - 2.0 * current)
        source = value_next + step_size * (hamilton + couple)
        current = jnp.einsum("wrsk,tk->wrst", source, tank_inverse, precision=lax.Precision.HIGHEST)
    action, hamilton = control_law(current, price)
    drift = jnp.swapaxes(action, 2, 3)
    upper, lower = neighbours(drift * density, 3)
    spread = 0.5 * (upper - lower)
    tank_up, tank_down = neighbours(density, 2)
    wind_up, wind_down = neighbours(density, 0)
    tank_term = tank_spread * (tank_up + tank_down - 2.0 * density)
    wind_term = wind_rate[:, :, None, None] * (wind_up + wind_down - 2.0 * density)
    source = density + step_size * (tank_term + wind_term - spread)
    density_next = jnp.einsum("wrks,ts->wrkt", source, soc_inverse, precision=lax.Precision.HIGHEST)
    return current, density_next
```

```python
import jax
import jax.numpy as jnp
from jax import lax
from jax.experimental import pallas as pl
from jax.experimental.pallas import tpu as pltpu
from jax.sharding import PartitionSpec as P

ITERS = 4
MESH = pl.DeviceIdType.MESH

step_size = 0.25
tank_spread = 0.3

F32 = jnp.float32
BF16 = jnp.bfloat16


def split(x):
    hi = x.astype(BF16)
    lo = (x - hi.astype(F32)).astype(BF16)
    return hi, lo


def body(
    price_s,
    rate_s,
    tinv_ref,
    sinv_ref,
    v_hbm,
    d_hbm,
    val_hbm,
    dn_hbm,
    u,
    x,
    rt,
    rs,
    pb,
    qb,
    d,
    dks,
    dkr,
    st,
    vo,
    sb,
    rb,
    ld_sem,
    st_sem,
    hs,
    hr,
    dhs,
    dhr,
    as_sem,
    ar_sem,
    own_sem,
):
    wi = lax.axis_index("wind")
    si = lax.axis_index("state")
    nw = 8
    ns = 16

    halves = (pl.ds(0, 128), pl.ds(128, 128))
    loads_v = [
        pltpu.make_async_copy(v_hbm.at[:, :, halves[kh]], st.at[kh], ld_sem.at[kh]) for kh in range(2)
    ]
    load_d = pltpu.make_async_copy(d_hbm, d.at[pl.ds(1, 16)], ld_sem.at[2])
    for load in loads_v:
        load.start()
    load_d.start()

    barrier = pltpu.get_barrier_semaphore()

    @pl.loop(1, ns)
    def _(p):
        pl.semaphore_signal(
            barrier, inc=1, device_id={"wind": wi, "state": (si + p) % ns}, device_id_type=MESH
        )

    @pl.when(wi > 0)
    def _():
        pl.semaphore_signal(barrier, inc=1, device_id={"wind": wi - 1, "state": si}, device_id_type=MESH)

    @pl.when(wi < nw - 1)
    def _():
        pl.semaphore_signal(barrier, inc=1, device_id={"wind": wi + 1, "state": si}, device_id_type=MESH)

    @pl.when(wi == 0)
    def _():
        d[0] = jnp.zeros((256, 256), F32)

        @pl.loop(0, ITERS)
        def _(n):
            for g in range(2):
                u[n, g, 0] = jnp.zeros((18, 8, 256), F32)

    @pl.when(wi == nw - 1)
    def _():
        d[17] = jnp.zeros((256, 256), F32)

        @pl.loop(0, ITERS)
        def _(n):
            for g in range(2):
                u[n, g, 17] = jnp.zeros((18, 8, 256), F32)

    @pl.when(si == 0)
    def _():
        dkr[0] = jnp.zeros((16, 16, 256), F32)

        @pl.loop(0, ITERS + 1)
        def _(n):
            for g in range(2):
                u[n, g, pl.ds(1, 16), 0] = jnp.zeros((16, 8, 256), F32)

    @pl.when(si == ns - 1)
    def _():
        dkr[1] = jnp.zeros((16, 16, 256), F32)

        @pl.loop(0, ITERS + 1)
        def _(n):
            for g in range(2):
                u[n, g, pl.ds(1, 16), 17] = jnp.zeros((16, 8, 256), F32)

    row = lax.broadcasted_iota(jnp.int32, (8, 128), 0)

    @pl.loop(0, 16)
    def _(w):
        for g in range(2):
            p = jnp.zeros((8, 128), F32)
            q = jnp.zeros((8, 128), F32)
            for r in range(8):
                p = jnp.where(row == r, price_s[w, g * 8 + r], p)
                q = jnp.where(row == r, rate_s[w, g * 8 + r], q)
            pb[g, w] = 0.5 * p
            qb[g, w] = step_size * q

    for inv_ref, out in ((tinv_ref, rt), (sinv_ref, rs)):
        hi, lo = split(inv_ref[...].T)
        out[pl.ds(0, 256)] = hi
        out[pl.ds(256, 256)] = lo

    expected = ns - 1 + jnp.where(wi > 0, 1, 0) + jnp.where(wi < nw - 1, 1, 0)
    pl.semaphore_wait(barrier, expected)

    def wind_copies(n, g):
        down = pltpu.make_async_remote_copy(
            src_ref=u.at[n, g, 1, pl.ds(1, 16)],
            dst_ref=u.at[n, g, 17, pl.ds(1, 16)],
            send_sem=hs.at[n, g, 0],
            recv_sem=hr.at[n, g, 0],
            device_id={"wind": wi - 1, "state": si},
            device_id_type=MESH,
        )
        up = pltpu.make_async_remote_copy(
            src_ref=u.at[n, g, 16, pl.ds(1, 16)],
            dst_ref=u.at[n, g, 0, pl.ds(1, 16)],
            send_sem=hs.at[n, g, 1],
            recv_sem=hr.at[n, g, 1],
            device_id={"wind": wi + 1, "state": si},
            device_id_type=MESH,
        )
        return down, up

    def state_copies(n, g):
        down = pltpu.make_async_remote_copy(
            src_ref=u.at[n, g, pl.ds(1, 16), 1],
            dst_ref=u.at[n, g, pl.ds(1, 16), 17],
            send_sem=hs.at[n, g, 2],
            recv_sem=hr.at[n, g, 2],
            device_id={"wind": wi, "state": si - 1},
            device_id_type=MESH,
        )
        up = pltpu.make_async_remote_copy(
            src_ref=u.at[n, g, pl.ds(1, 16), 16],
            dst_ref=u.at[n, g, pl.ds(1, 16), 0],
            send_sem=hs.at[n, g, 3],
            recv_sem=hr.at[n, g, 3],
            device_id={"wind": wi, "state": si + 1},
            device_id_type=MESH,
        )
        return down, up

    def dens_wind_copies():
        down = pltpu.make_async_remote_copy(
            src_ref=d_hbm.at[0],
            dst_ref=d.at[17],
            send_sem=dhs.at[0],
            recv_sem=dhr.at[0],
            device_id={"wind": wi - 1, "state": si},
            device_id_type=MESH,
        )
        up = pltpu.make_async_remote_copy(
            src_ref=d_hbm.at[15],
            dst_ref=d.at[0],
            send_sem=dhs.at[1],
            recv_sem=dhr.at[1],
            device_id={"wind": wi + 1, "state": si},
            device_id_type=MESH,
        )
        return down, up

    def dens_state_copies():
        down = pltpu.make_async_remote_copy(
            src_ref=dks.at[0],
            dst_ref=dkr.at[1],
            send_sem=dhs.at[2],
            recv_sem=dhr.at[2],
            device_id={"wind": wi, "state": si - 1},
            device_id_type=MESH,
        )
        up = pltpu.make_async_remote_copy(
            src_ref=dks.at[1],
            dst_ref=dkr.at[0],
            send_sem=dhs.at[3],
            recv_sem=dhr.at[3],
            device_id={"wind": wi, "state": si + 1},
            device_id_type=MESH,
        )
        return down, up

    def start(pair, index, last):
        @pl.when(index > 0)
        def _():
            pair[0].start()

        @pl.when(index < last)
        def _():
            pair[1].start()

    def arrive(pair, index, last):
        @pl.when(index < last)
        def _():
            pair[0].wait_recv()

        @pl.when(index > 0)
        def _():
            pair[1].wait_recv()

    def drain(pair, index, last):
        @pl.when(index > 0)
        def _():
            pair[0].wait_send()

        @pl.when(index < last)
        def _():
            pair[1].wait_send()

    start(dens_wind_copies(), wi, nw - 1)

    for load in loads_v:
        load.wait()
    for g in range(2):

        @pl.loop(0, 16)
        def _(w):
            for s in range(16):
                for kh in range(2):
                    u[0, g, w + 1, s + 1, :, halves[kh]] = st[kh, w, pl.ds(g * 128 + s, 8, stride=16), :]

        start(wind_copies(0, g), wi, nw - 1)
        start(state_copies(0, g), si, ns - 1)

    load_d.wait()

    @pl.loop(0, 16)
    def _(w):
        for r in range(16):
            dks[0, w, pl.ds(r, 1), :] = d[w + 1, pl.ds(r * 16, 1), :]
            dks[1, w, pl.ds(r, 1), :] = d[w + 1, pl.ds(r * 16 + 15, 1), :]

    def matmul(r):
        return (
            jnp.dot(x[:, pl.ds(0, 256)], r[pl.ds(0, 256)], preferred_element_type=F32)
            + jnp.dot(x[:, pl.ds(256, 256)], r[pl.ds(0, 256)], preferred_element_type=F32)
            + jnp.dot(x[:, pl.ds(0, 256)], r[pl.ds(256, 256)], preferred_element_type=F32)
        )

    def both(tile):
        return jnp.concatenate([tile, tile], axis=1)[None]

    @pl.loop(0, 2 * ITERS)
    def _(m):
        n = m // 2
        g = m % 2
        arrive(wind_copies(n, g), wi, nw - 1)
        arrive(state_copies(n, g), si, ns - 1)

        @pl.loop(0, 4)
        def _(c):
            @pl.loop(0, 4)
            def _(j):
                w = c * 4 + j
                half = 0.25 * (u[n, g, w + 1, pl.ds(2, 16)] - u[n, g, w + 1, pl.ds(0, 16)]) + both(pb[g, w])
                t = jnp.tanh(half)
                mid = u[n, g, w + 1, pl.ds(1, 16)]
                couple = u[n, g, w + 2, pl.ds(1, 16)] + u[n, g, w, pl.ds(1, 16)] - 2.0 * mid
                source = (
                    u[0, g, w + 1, pl.ds(1, 16)] + 0.5 * t * (t - 2.0 * half) + both(qb[g, w]) * couple
                )
                hi, lo = split(source.reshape(128, 256))
                rows = pl.ds(pl.multiple_of(j * 128, 128), 128)
                x[rows, pl.ds(0, 256)] = hi
                x[rows, pl.ds(256, 256)] = lo

            u[n + 1, g, pl.ds(c * 4 + 1, 4), pl.ds(1, 16)] = matmul(rt).reshape(4, 16, 8, 256)

        @pl.when(n < ITERS - 1)
        def _():
            start(wind_copies(n + 1, g), wi, nw - 1)

        start(state_copies(n + 1, g), si, ns - 1)

        @pl.when(m == 1)
        def _():
            start(dens_state_copies(), si, ns - 1)

    group = lax.broadcasted_iota(jnp.int32, (8, 128), 1) // 16

    def own_copy(g, h):
        return pltpu.make_async_copy(sb.at[g, h, si], rb.at[g, h, si], own_sem.at[g, h])

    @pl.loop(0, 4)
    def _(m):
        g = m // 2
        h = m % 2

        @pl.when(h == 0)
        def _():
            arrive(state_copies(ITERS, g), si, ns - 1)

        @pl.loop(0, 16)
        def _(s):
            for kh in range(2):
                lanes = pl.ds(kh * 128, 128)
                a = []
                for w in range(8):
                    slot = h * 8 + w
                    half = (
                        0.25 * (u[ITERS, g, slot + 1, s + 2, :, lanes] - u[ITERS, g, slot + 1, s, :, lanes])
                        + pb[g, slot]
                    )
                    a.append(-2.0 * jnp.tanh(half))
                for bit in (4, 2, 1):
                    high = (group // bit) % 2 == 1
                    b = [None] * 8
                    for w in range(8):
                        if w & bit == 0:
                            b[w] = jnp.where(high, pltpu.roll(a[w + bit], 16 * bit, 1), a[w])
                            b[w + bit] = jnp.where(high, a[w + bit], pltpu.roll(a[w], 128 - 16 * bit, 1))
                    a = b
                for w in range(8):
                    sb[g, h, kh * 8 + w, pl.ds(pl.multiple_of(s * 8, 8), 8), :] = a[w]

        own_copy(g, h).start()

        @pl.loop(1, ns)
        def _(p):
            to = (si + p) % ns
            pltpu.make_async_remote_copy(
                src_ref=sb.at[g, h, to],
                dst_ref=rb.at[g, h, si],
                send_sem=as_sem.at[g, h],
                recv_sem=ar_sem.at[g, h],
                device_id={"wind": wi, "state": to},
                device_id_type=MESH,
            ).start()

    @pl.loop(0, 16)
    def _(w):
        for g in range(2):
            for s in range(16):
                for kh in range(2):
                    vo[kh, w, pl.ds(g * 128 + s, 8, stride=16), :] = u[ITERS, g, w + 1, s + 1, :, halves[kh]]

    stores_v = [
        pltpu.make_async_copy(vo.at[kh], val_hbm.at[:, :, halves[kh]], st_sem.at[4, kh]) for kh in range(2)
    ]
    for store in stores_v:
        store.start()

    arrive(dens_wind_copies(), wi, nw - 1)
    arrive(dens_state_copies(), si, ns - 1)
    level = lax.broadcasted_iota(jnp.int32, (16, 256), 0)

    @pl.loop(0, 16)
    def _(w):
        @pl.loop(0, 16)
        def _(r):
            rows = pl.ds(pl.multiple_of(r * 16, 16), 16)
            mid = d[w + 1, rows, :]
            above = jnp.where(level == 15, dkr[1, w, pl.ds(r, 1), :], pltpu.roll(mid, 15, 0))
            below = jnp.where(level == 0, dkr[0, w, pl.ds(r, 1), :], pltpu.roll(mid, 1, 0))
            couple = d[w + 2, rows, :] + d[w, rows, :] - 2.0 * mid
            source = (
                mid
                + (step_size * tank_spread) * (above + below - 2.0 * mid)
                + (step_size * rate_s[w, r]) * couple
            )
            for kh in range(2):
                st[kh, w, rows, :] = source[:, kh * 128 : (kh + 1) * 128]

    point = lax.broadcasted_iota(jnp.int32, (128, 256), 1)

    def stores_d(g, h):
        rooms = pl.ds(pl.multiple_of(g * 128, 128), 128)
        return [
            pltpu.make_async_copy(
                st.at[kh, pl.ds(h * 8, 8), rooms],
                dn_hbm.at[pl.ds(h * 8, 8), rooms, halves[kh]],
                st_sem.at[g * 2 + h, kh],
            )
            for kh in range(2)
        ]

    def all_blocks(ref, g, h, sem):
        blocks = ref.at[g, h, pl.ds(0, ns - 1)]
        return pltpu.make_async_copy(blocks, blocks, sem.at[g, h])

    @pl.loop(0, 4)
    def _(m):
        g = m // 2
        h = m % 2
        own_copy(g, h).wait()
        all_blocks(rb, g, h, ar_sem).wait()

        @pl.loop(0, 2)
        def _(c):
            @pl.loop(0, 4)
            def _(j):
                r = c * 4 + j
                rows = pl.ds(pl.multiple_of((g * 8 + r) * 16, 16), 16)
                blocks = [rb[g, h, i, pl.ds(r, 16, stride=8), :] for i in range(ns)]
                drift = jnp.concatenate(blocks, axis=0).T
                flux = drift * d[pl.ds(1 + h * 8, 8), rows, :].reshape(128, 256)
                upper = jnp.where(point == 255, 0.0, pltpu.roll(flux, 255, 1))
                lower = jnp.where(point == 0, 0.0, pltpu.roll(flux, 1, 1))
                still = jnp.concatenate(
                    [st[kh, pl.ds(h * 8, 8), rows, :].reshape(128, 128) for kh in range(2)], axis=1
                )
                source = still - (0.5 * step_size) * (upper - lower)
                hi, lo = split(source)
                at = pl.ds(pl.multiple_of(j * 128, 128), 128)
                x[at, pl.ds(0, 256)] = hi
                x[at, pl.ds(256, 256)] = lo

            out = matmul(rs)
            for j in range(4):
                rows = pl.ds(pl.multiple_of((g * 8 + c * 4 + j) * 16, 16), 16)
                for kh in range(2):
                    st[kh, pl.ds(h * 8, 8), rows, :] = out[
                        j * 128 : (j + 1) * 128, kh * 128 : (kh + 1) * 128
                    ].reshape(8, 16, 128)

        for store in stores_d(g, h):
            store.start()

    @pl.loop(0, 4)
    def _(m):
        g = m // 2
        h = m % 2
        all_blocks(sb, g, h, as_sem).wait()
        for store in stores_d(g, h):
            store.wait()

    @pl.loop(0, 2 * ITERS)
    def _(m):
        n = m // 2
        g = m % 2
        drain(wind_copies(n, g), wi, nw - 1)

    @pl.loop(0, 2 * (ITERS + 1))
    def _(m):
        n = m // 2
        g = m % 2
        drain(state_copies(n, g), si, ns - 1)

    drain(dens_wind_copies(), wi, nw - 1)
    drain(dens_state_copies(), si, ns - 1)
    for store in stores_v:
        store.wait()


def on_device(value_next, density, price, wind_rate, tank_inverse, soc_inverse):
    flat = (16, 256, 256)
    smem = pl.BlockSpec(memory_space=pltpu.SMEM)
    vmem = pl.BlockSpec(memory_space=pltpu.VMEM)
    hbm = pl.BlockSpec(memory_space=pl.ANY)
    dma = pltpu.SemaphoreType.DMA
    value, dens = pl.pallas_call(
        body,
        name="storage_step",
        out_shape=(jax.ShapeDtypeStruct(flat, F32), jax.ShapeDtypeStruct(flat, F32)),
        in_specs=[smem, smem, vmem, vmem, hbm, hbm],
        out_specs=(hbm, hbm),
        scratch_shapes=[
            pltpu.VMEM((ITERS + 1, 2, 18, 18, 8, 256), F32),
            pltpu.VMEM((512, 512), BF16),
            pltpu.VMEM((512, 256), BF16),
            pltpu.VMEM((512, 256), BF16),
            pltpu.VMEM((2, 16, 8, 128), F32),
            pltpu.VMEM((2, 16, 8, 128), F32),
            pltpu.VMEM((18, 256, 256), F32),
            pltpu.VMEM((2, 16, 16, 256), F32),
            pltpu.VMEM((2, 16, 16, 256), F32),
            pltpu.VMEM((2, 16, 256, 128), F32),
            pltpu.VMEM((2, 16, 256, 128), F32),
            pltpu.VMEM((2, 2, 16, 128, 128), F32),
            pltpu.VMEM((2, 2, 16, 128, 128), F32),
            dma((3,)),
            dma((5, 2)),
            dma((ITERS + 1, 2, 4)),
            dma((ITERS + 1, 2, 4)),
            dma((4,)),
            dma((4,)),
            dma((2, 2)),
            dma((2, 2)),
            dma((2, 2)),
        ],
        compiler_params=pltpu.CompilerParams(
            collective_id=0, has_side_effects=True, vmem_limit_bytes=62 * 1024 * 1024
        ),
    )(price, wind_rate, tank_inverse, soc_inverse, value_next.reshape(flat), density.reshape(flat))
    return value.reshape(value_next.shape), dens.reshape(density.shape)


def solution(mesh):
    placed = (
        P("wind", None, "state", None),
        P("wind", None, "state", None),
        P("wind", None),
        P("wind", None),
        P(),
        P(),
    )
    return jax.shard_map(
        on_device,
        mesh=mesh,
        in_specs=placed,
        out_specs=(P("wind", None, "state", None), P("wind", None, "state", None)),
        check_vma=False,
    )
```

```python
import jax
import jax.numpy as jnp
from jax import lax
from jax.experimental import pallas as pl
from jax.experimental.pallas import tpu as pltpu
from jax.sharding import PartitionSpec as P

ITERS = 4
MESH = pl.DeviceIdType.MESH

step_size = 0.25
tank_spread = 0.3

F32 = jnp.float32
BF16 = jnp.bfloat16


def split(x):
    hi = x.astype(BF16)
    lo = (x - hi.astype(F32)).astype(BF16)
    return hi, lo


def body(
    price_hbm,
    rate_hbm,
    tinv_hbm,
    sinv_hbm,
    v_hbm,
    d_hbm,
    vo,
    do,
    u,
    uf,
    x,
    rt,
    rs,
    pb,
    qb,
    d,
    dks,
    dkr,
    pc,
    sb,
    rb,
    price_s,
    rate_s,
    inv,
    ld_sem,
    hs,
    hr,
    dhs,
    dhr,
    as_sem,
    ar_sem,
    own_sem,
):
    wi = lax.axis_index("wind")
    si = lax.axis_index("state")
    nw = 8
    ns = 16

    halves = (pl.ds(0, 128), pl.ds(128, 128))
    load_v = pltpu.make_async_copy(v_hbm, vo, ld_sem.at[0])
    load_d = pltpu.make_async_copy(d_hbm, d.at[pl.ds(1, 16)], ld_sem.at[1])
    load_v.start()
    load_d.start()
    small = [
        pltpu.make_async_copy(src, dst, ld_sem.at[2 + i])
        for i, (src, dst) in enumerate(
            ((price_hbm, price_s), (rate_hbm, rate_s), (tinv_hbm, inv.at[0]), (sinv_hbm, inv.at[1]))
        )
    ]
    for load in small:
        load.start()

    barrier = pltpu.get_barrier_semaphore()

    @pl.loop(1, ns)
    def _(p):
        pl.semaphore_signal(
            barrier, inc=1, device_id={"wind": wi, "state": (si + p) % ns}, device_id_type=MESH
        )

    @pl.when(wi > 0)
    def _():
        pl.semaphore_signal(barrier, inc=1, device_id={"wind": wi - 1, "state": si}, device_id_type=MESH)

    @pl.when(wi < nw - 1)
    def _():
        pl.semaphore_signal(barrier, inc=1, device_id={"wind": wi + 1, "state": si}, device_id_type=MESH)

    @pl.when(wi == 0)
    def _():
        d[0] = jnp.zeros((256, 256), F32)

        @pl.loop(0, ITERS)
        def _(n):
            for g in range(2):
                u[n, g, 0] = jnp.zeros((18, 8, 256), F32)

    @pl.when(wi == nw - 1)
    def _():
        d[17] = jnp.zeros((256, 256), F32)

        @pl.loop(0, ITERS)
        def _(n):
            for g in range(2):
                u[n, g, 17] = jnp.zeros((18, 8, 256), F32)

    @pl.when(si == 0)
    def _():
        dkr[0] = jnp.zeros((16, 16, 256), F32)

        @pl.loop(0, ITERS)
        def _(n):
            for g in range(2):
                u[n, g, pl.ds(1, 16), 0] = jnp.zeros((16, 8, 256), F32)

    @pl.when(si == ns - 1)
    def _():
        dkr[1] = jnp.zeros((16, 16, 256), F32)

        @pl.loop(0, ITERS)
        def _(n):
            for g in range(2):
                u[n, g, pl.ds(1, 16), 17] = jnp.zeros((16, 8, 256), F32)

    expected = ns - 1 + jnp.where(wi > 0, 1, 0) + jnp.where(wi < nw - 1, 1, 0)
    pl.semaphore_wait(barrier, expected)

    def wind_copies(n, g):
        down = pltpu.make_async_remote_copy(
            src_ref=u.at[n, g, 1, pl.ds(1, 16)],
            dst_ref=u.at[n, g, 17, pl.ds(1, 16)],
            send_sem=hs.at[n, g, 0],
            recv_sem=hr.at[n, g, 0],
            device_id={"wind": wi - 1, "state": si},
            device_id_type=MESH,
        )
        up = pltpu.make_async_remote_copy(
            src_ref=u.at[n, g, 16, pl.ds(1, 16)],
            dst_ref=u.at[n, g, 0, pl.ds(1, 16)],
            send_sem=hs.at[n, g, 1],
            recv_sem=hr.at[n, g, 1],
            device_id={"wind": wi + 1, "state": si},
            device_id_type=MESH,
        )
        return down, up

    def state_copies(n, g):
        down = pltpu.make_async_remote_copy(
            src_ref=u.at[n, g, pl.ds(1, 16), 1],
            dst_ref=u.at[n, g, pl.ds(1, 16), 17],
            send_sem=hs.at[n, g, 2],
            recv_sem=hr.at[n, g, 2],
            device_id={"wind": wi, "state": si - 1},
            device_id_type=MESH,
        )
        up = pltpu.make_async_remote_copy(
            src_ref=u.at[n, g, pl.ds(1, 16), 16],
            dst_ref=u.at[n, g, pl.ds(1, 16), 0],
            send_sem=hs.at[n, g, 3],
            recv_sem=hr.at[n, g, 3],
            device_id={"wind": wi, "state": si + 1},
            device_id_type=MESH,
        )
        return down, up

    def dens_wind_copies():
        down = pltpu.make_async_remote_copy(
            src_ref=d_hbm.at[0],
            dst_ref=d.at[17],
            send_sem=dhs.at[0],
            recv_sem=dhr.at[0],
            device_id={"wind": wi - 1, "state": si},
            device_id_type=MESH,
        )
        up = pltpu.make_async_remote_copy(
            src_ref=d_hbm.at[15],
            dst_ref=d.at[0],
            send_sem=dhs.at[1],
            recv_sem=dhr.at[1],
            device_id={"wind": wi + 1, "state": si},
            device_id_type=MESH,
        )
        return down, up

    def dens_state_copies():
        down = pltpu.make_async_remote_copy(
            src_ref=dks.at[0],
            dst_ref=dkr.at[1],
            send_sem=dhs.at[2],
            recv_sem=dhr.at[2],
            device_id={"wind": wi, "state": si - 1},
            device_id_type=MESH,
        )
        up = pltpu.make_async_remote_copy(
            src_ref=dks.at[1],
            dst_ref=dkr.at[0],
            send_sem=dhs.at[3],
            recv_sem=dhr.at[3],
            device_id={"wind": wi, "state": si + 1},
            device_id_type=MESH,
        )
        return down, up

    def start(pair, index, last):
        @pl.when(index > 0)
        def _():
            pair[0].start()

        @pl.when(index < last)
        def _():
            pair[1].start()

    def arrive(pair, index, last):
        @pl.when(index < last)
        def _():
            pair[0].wait_recv()

        @pl.when(index > 0)
        def _():
            pair[1].wait_recv()

    def drain(pair, index, last):
        @pl.when(index > 0)
        def _():
            pair[0].wait_send()

        @pl.when(index < last)
        def _():
            pair[1].wait_send()

    start(dens_wind_copies(), wi, nw - 1)

    def tile_rows(g, s, kh):
        return pl.ds(g * 256 + (s // 8) * 16 + kh * 8 + s % 8, 8, stride=32)

    load_v.wait()
    for g in range(2):

        @pl.loop(0, 16)
        def _(w):
            for s in range(16):
                for kh in range(2):
                    u[0, g, w + 1, s + 1, :, halves[kh]] = vo[w, tile_rows(g, s, kh), :]

        start(wind_copies(0, g), wi, nw - 1)
        start(state_copies(0, g), si, ns - 1)

    load_d.wait()

    @pl.loop(0, 16)
    def _(w):
        for r in range(16):
            dks[0, w, pl.ds(r, 1), :] = d[w + 1, pl.ds(r * 16, 1), :]
            dks[1, w, pl.ds(r, 1), :] = d[w + 1, pl.ds(r * 16 + 15, 1), :]

    for load in small:
        load.wait()
    row = lax.broadcasted_iota(jnp.int32, (8, 128), 0)

    @pl.loop(0, 16)
    def _(w):
        for g in range(2):
            p = jnp.zeros((8, 128), F32)
            q = jnp.zeros((8, 128), F32)
            for r in range(8):
                p = jnp.where(row == r, price_s[w, g * 8 + r], p)
                q = jnp.where(row == r, rate_s[w, g * 8 + r], q)
            pb[g, w] = 0.5 * p
            qb[g, w] = step_size * q

    group = lax.broadcasted_iota(jnp.int32, (8, 128), 1) // 16
    for g in range(2):
        for h in range(2):
            rb[g, h, pl.ds(0, 8), :] = jnp.zeros((8, 128), F32)
            rb[g, h, pl.ds(2056, 8), :] = jnp.zeros((8, 128), F32)

            @pl.loop(0, 8)
            def _(r):
                p = jnp.zeros((1, 128), F32)
                for w in range(8):
                    p = jnp.where(group[:1] == w, 0.5 * price_s[h * 8 + w, g * 8 + r], p)
                pc[g, h, pl.ds(r, 1), :] = p

    for i, out in enumerate((rt, rs)):
        hi, lo = split(inv[i].T)
        out[pl.ds(0, 256)] = hi
        out[pl.ds(256, 256)] = lo

    def matmul(r):
        return (
            jnp.dot(x[:, pl.ds(0, 256)], r[pl.ds(0, 256)], preferred_element_type=F32)
            + jnp.dot(x[:, pl.ds(256, 256)], r[pl.ds(0, 256)], preferred_element_type=F32)
            + jnp.dot(x[:, pl.ds(0, 256)], r[pl.ds(256, 256)], preferred_element_type=F32)
        )

    def both(tile):
        return jnp.concatenate([tile, tile], axis=1)[None]

    def own_copy(g, h):
        return pltpu.make_async_copy(
            sb.at[g, h, si], rb.at[g, h, pl.ds(pl.multiple_of(8 + si * 128, 8), 128)], own_sem.at[g, h]
        )

    def regroup(g, h):
        @pl.loop(0, 4)
        def _(quad):
            for i in range(4):
                s = quad * 4 + i
                for kh in range(2):
                    a = [uf[g, h * 8 + w, s, :, halves[kh]] for w in range(8)]
                    for bit in (4, 2, 1):
                        high = (group // bit) % 2 == 1
                        b = [None] * 8
                        for w in range(8):
                            if w & bit == 0:
                                b[w] = jnp.where(high, pltpu.roll(a[w + bit], 16 * bit, 1), a[w])
                                b[w + bit] = jnp.where(high, a[w + bit], pltpu.roll(a[w], 128 - 16 * bit, 1))
                        a = b
                    for w in range(8):
                        sb[g, h, kh * 8 + w, pl.ds(pl.multiple_of(s * 8, 8), 8), :] = a[w]

    def send(g, h):
        own_copy(g, h).start()

        @pl.loop(1, ns)
        def _(p):
            to = (si + p) % ns
            pltpu.make_async_remote_copy(
                src_ref=sb.at[g, h, to],
                dst_ref=rb.at[g, h, pl.ds(pl.multiple_of(8 + si * 128, 8), 128)],
                send_sem=as_sem.at[g, h],
                recv_sem=ar_sem.at[g, h],
                device_id={"wind": wi, "state": to},
                device_id_type=MESH,
            ).start()

    @pl.loop(0, 2 * ITERS)
    def _(m):
        n = m // 2
        g = m % 2
        arrive(wind_copies(n, g), wi, nw - 1)
        arrive(state_copies(n, g), si, ns - 1)
        @pl.when(m == 2 * ITERS - 1)
        def _():
            for h in range(2):
                send(0, h)


        @pl.loop(0, 4)
        def _(c):
            @pl.loop(0, 4)
            def _(j):
                w = c * 4 + j
                half = 0.25 * (u[n, g, w + 1, pl.ds(2, 16)] - u[n, g, w + 1, pl.ds(0, 16)]) + both(pb[g, w])
                t = jnp.tanh(half)
                mid = u[n, g, w + 1, pl.ds(1, 16)]
                couple = u[n, g, w + 2, pl.ds(1, 16)] + u[n, g, w, pl.ds(1, 16)] - 2.0 * mid
                source = (
                    u[0, g, w + 1, pl.ds(1, 16)] + 0.5 * t * (t - 2.0 * half) + both(qb[g, w]) * couple
                )
                hi, lo = split(source.reshape(128, 256))
                rows = pl.ds(pl.multiple_of(j * 128, 128), 128)
                x[rows, pl.ds(0, 256)] = hi
                x[rows, pl.ds(256, 256)] = lo

            swept = matmul(rt).reshape(4, 16, 8, 256)

            @pl.when(n < ITERS - 1)
            def _():
                u[n + 1, g, pl.ds(c * 4 + 1, 4), pl.ds(1, 16)] = swept

            @pl.when(n == ITERS - 1)
            def _():
                uf[g, pl.ds(c * 4, 4)] = swept

        @pl.when(n < ITERS - 1)
        def _():
            start(wind_copies(n + 1, g), wi, nw - 1)
            start(state_copies(n + 1, g), si, ns - 1)

        @pl.when(m == 1)
        def _():
            start(dens_state_copies(), si, ns - 1)

        @pl.when(n == ITERS - 1)
        def _():
            for h in range(2):
                regroup(g, h)

            @pl.when(g == 1)
            def _():
                for h in range(2):
                    send(1, h)

    @pl.loop(0, 16)
    def _(w):
        for g in range(2):
            for s in range(16):
                for kh in range(2):
                    vo[w, tile_rows(g, s, kh), :] = uf[g, w, s, :, halves[kh]]

    arrive(dens_wind_copies(), wi, nw - 1)
    arrive(dens_state_copies(), si, ns - 1)
    level = lax.broadcasted_iota(jnp.int32, (16, 256), 0)

    @pl.loop(0, 16)
    def _(w):
        @pl.loop(0, 16)
        def _(r):
            rows = pl.ds(pl.multiple_of(r * 16, 16), 16)
            mid = d[w + 1, rows, :]
            above = jnp.where(level == 15, dkr[1, w, pl.ds(r, 1), :], pltpu.roll(mid, 15, 0))
            below = jnp.where(level == 0, dkr[0, w, pl.ds(r, 1), :], pltpu.roll(mid, 1, 0))
            couple = d[w + 2, rows, :] + d[w, rows, :] - 2.0 * mid
            source = (
                mid
                + (step_size * tank_spread) * (above + below - 2.0 * mid)
                + (step_size * rate_s[w, r]) * couple
            )
            for kh in range(2):
                do[w, pl.ds(r * 2, 2), kh] = source[:, kh * 128 : (kh + 1) * 128].reshape(2, 8, 128)

    point = lax.broadcasted_iota(jnp.int32, (128, 256), 1)

    def all_blocks(g, h, sem):
        blocks = sb.at[g, h, pl.ds(0, ns - 1)]
        return pltpu.make_async_copy(blocks, blocks, sem.at[g, h])

    @pl.loop(0, 4)
    def _(m):
        g = m // 2
        h = m % 2
        own_copy(g, h).wait()
        all_blocks(g, h, ar_sem).wait()

        @pl.loop(0, 2)
        def _(c):
            @pl.loop(0, 4)
            def _(j):
                r = c * 4 + j
                rows = pl.ds(pl.multiple_of((g * 8 + r) * 16, 16), 16)
                tiles = pl.ds((g * 8 + r) * 2, 2)
                above = rb[g, h, pl.ds(r + 16, 256, stride=8), :]
                below = rb[g, h, pl.ds(r, 256, stride=8), :]
                drift = (-2.0 * jnp.tanh(0.25 * (above - below) + pc[g, h, pl.ds(r, 1), :])).T
                flux = drift * d[pl.ds(1 + h * 8, 8), rows, :].reshape(128, 256)
                upper = jnp.where(point == 255, 0.0, pltpu.roll(flux, 255, 1))
                lower = jnp.where(point == 0, 0.0, pltpu.roll(flux, 1, 1))
                still = jnp.concatenate(
                    [do[pl.ds(h * 8, 8), tiles, kh].reshape(128, 128) for kh in range(2)], axis=1
                )
                source = still - (0.5 * step_size) * (upper - lower)
                hi, lo = split(source)
                at = pl.ds(pl.multiple_of(j * 128, 128), 128)
                x[at, pl.ds(0, 256)] = hi
                x[at, pl.ds(256, 256)] = lo

            out = matmul(rs)
            for j in range(4):
                tiles = pl.ds((g * 8 + c * 4 + j) * 2, 2)
                for kh in range(2):
                    do[pl.ds(h * 8, 8), tiles, kh] = out[
                        j * 128 : (j + 1) * 128, kh * 128 : (kh + 1) * 128
                    ].reshape(8, 2, 8, 128)

    @pl.loop(0, 4)
    def _(m):
        g = m // 2
        h = m % 2
        all_blocks(g, h, as_sem).wait()

    @pl.loop(0, 2 * ITERS)
    def _(m):
        n = m // 2
        g = m % 2
        drain(wind_copies(n, g), wi, nw - 1)
        drain(state_copies(n, g), si, ns - 1)

    drain(dens_wind_copies(), wi, nw - 1)
    drain(dens_state_copies(), si, ns - 1)


def on_device(value_next, density, price, wind_rate, tank_inverse, soc_inverse):
    vmem = pl.BlockSpec(memory_space=pltpu.VMEM)
    hbm = pl.BlockSpec(memory_space=pltpu.HBM)
    dma = pltpu.SemaphoreType.DMA
    tiles = value_next.reshape(16, 32, 8, 2, 128).transpose(0, 1, 3, 2, 4).reshape(16, 512, 128)
    value, dens = pl.pallas_call(
        body,
        name="storage_step",
        out_shape=(
            jax.ShapeDtypeStruct((16, 512, 128), F32),
            jax.ShapeDtypeStruct((16, 32, 2, 8, 128), F32),
        ),
        in_specs=[hbm] * 6,
        out_specs=(vmem, vmem),
        scratch_shapes=[
            pltpu.VMEM((ITERS, 2, 18, 18, 8, 256), F32),
            pltpu.VMEM((2, 16, 16, 8, 256), F32),
            pltpu.VMEM((512, 512), BF16),
            pltpu.VMEM((512, 256), BF16),
            pltpu.VMEM((512, 256), BF16),
            pltpu.VMEM((2, 16, 8, 128), F32),
            pltpu.VMEM((2, 16, 8, 128), F32),
            pltpu.VMEM((18, 256, 256), F32),
            pltpu.VMEM((2, 16, 16, 256), F32),
            pltpu.VMEM((2, 16, 16, 256), F32),
            pltpu.VMEM((2, 2, 8, 128), F32),
            pltpu.VMEM((2, 2, 16, 128, 128), F32),
            pltpu.VMEM((2, 2, 2064, 128), F32),
            pltpu.SMEM((16, 16), F32),
            pltpu.SMEM((16, 16), F32),
            pltpu.VMEM((2, 256, 256), F32),
            dma((6,)),
            dma((ITERS, 2, 4)),
            dma((ITERS, 2, 4)),
            dma((4,)),
            dma((4,)),
            dma((2, 2)),
            dma((2, 2)),
            dma((2, 2)),
        ],
        compiler_params=pltpu.CompilerParams(
            collective_id=0, has_side_effects=True, vmem_limit_bytes=42 * 1024 * 1024
        ),
    )(*[pltpu.with_memory_space_constraint(a, pltpu.HBM) for a in (price, wind_rate, tank_inverse, soc_inverse, tiles, density.reshape(16, 256, 256))])

    def whole(out):
        return out.reshape(16, 32, 2, 8, 128).transpose(0, 1, 3, 2, 4).reshape(16, 16, 16, 256)

    return whole(value), whole(dens)


def solution(mesh):
    placed = (
        P("wind", None, "state", None),
        P("wind", None, "state", None),
        P("wind", None),
        P("wind", None),
        P(),
        P(),
    )
    return jax.shard_map(
        on_device,
        mesh=mesh,
        in_specs=placed,
        out_specs=(P("wind", None, "state", None), P("wind", None, "state", None)),
        check_vma=False,
    )
```

```python
import jax
import jax.numpy as jnp
from jax import lax
from jax.experimental import pallas as pl
from jax.experimental.pallas import tpu as pltpu
from jax.sharding import PartitionSpec as P

ITERS = 4
MESH = pl.DeviceIdType.MESH

step_size = 0.25
tank_spread = 0.3

F32 = jnp.float32
BF16 = jnp.bfloat16


def split(x):
    hi = x.astype(BF16)
    lo = (x - hi.astype(F32)).astype(BF16)
    return hi, lo


def body(
    price_hbm,
    rate_hbm,
    tinv_hbm,
    sinv_hbm,
    v_hbm,
    d_hbm,
    vo,
    do,
    u,
    uf,
    x,
    rt,
    rs,
    pb,
    qb,
    d,
    dks,
    dkr,
    pc,
    sb,
    rb,
    price_s,
    rate_s,
    inv,
    held,
    held_d,
    ld_sem,
    hs,
    hr,
    ss,
    sr,
    dhs,
    dhr,
    dss,
    dsr,
    as_sem,
    ar_sem,
    own_sem,
    rl,
    fs,
):
    wi = lax.axis_index("wind")
    si = lax.axis_index("state")
    nw = 8
    ns = 16

    halves = (pl.ds(0, 128), pl.ds(128, 128))
    load_v = pltpu.make_async_copy(v_hbm, vo, ld_sem.at[0])
    load_d = pltpu.make_async_copy(d_hbm, d.at[pl.ds(1, 16)], ld_sem.at[1])
    load_v.start()
    load_d.start()
    small = [
        pltpu.make_async_copy(src, dst, ld_sem.at[2 + i])
        for i, (src, dst) in enumerate(
            ((price_hbm, price_s), (rate_hbm, rate_s), (tinv_hbm, inv.at[0]), (sinv_hbm, inv.at[1]))
        )
    ]
    for load in small:
        load.start()

    barrier = pltpu.get_barrier_semaphore()

    @pl.loop(1, ns)
    def _(p):
        pl.semaphore_signal(
            barrier, inc=1, device_id={"wind": wi, "state": (si + p) % ns}, device_id_type=MESH
        )

    @pl.when(wi > 0)
    def _():
        pl.semaphore_signal(barrier, inc=1, device_id={"wind": wi - 1, "state": si}, device_id_type=MESH)

    @pl.when(wi < nw - 1)
    def _():
        pl.semaphore_signal(barrier, inc=1, device_id={"wind": wi + 1, "state": si}, device_id_type=MESH)

    @pl.when(wi == 0)
    def _():
        d[0] = jnp.zeros((256, 256), F32)

        @pl.loop(0, ITERS)
        def _(n):
            for g in range(2):
                u[n, g, 0] = jnp.zeros((18, 8, 256), F32)

    @pl.when(wi == nw - 1)
    def _():
        d[17] = jnp.zeros((256, 256), F32)

        @pl.loop(0, ITERS)
        def _(n):
            for g in range(2):
                u[n, g, 17] = jnp.zeros((18, 8, 256), F32)

    @pl.when(si == 0)
    def _():
        dkr[0] = jnp.zeros((16, 16, 256), F32)

        @pl.loop(0, ITERS)
        def _(n):
            for g in range(2):
                u[n, g, pl.ds(1, 16), 0] = jnp.zeros((16, 8, 256), F32)

    @pl.when(si == ns - 1)
    def _():
        dkr[1] = jnp.zeros((16, 16, 256), F32)

        @pl.loop(0, ITERS)
        def _(n):
            for g in range(2):
                u[n, g, pl.ds(1, 16), 17] = jnp.zeros((16, 8, 256), F32)

    @pl.when(wi >= 2)
    def _():
        pl.semaphore_signal(barrier, inc=1, device_id={"wind": wi - 2, "state": si}, device_id_type=MESH)

    @pl.when(wi < nw - 2)
    def _():
        pl.semaphore_signal(barrier, inc=1, device_id={"wind": wi + 2, "state": si}, device_id_type=MESH)

    expected = ns - 1
    for near in (wi > 0, wi < nw - 1, wi >= 2, wi < nw - 2):
        expected = expected + jnp.where(near, 1, 0)
    pl.semaphore_wait(barrier, expected)

    def wind_part(n, g, up, k):
        points = pl.ds(1 + 4 * k, 4)
        return pltpu.make_async_remote_copy(
            src_ref=u.at[n, g, 16 if up else 1, points],
            dst_ref=u.at[n, g, 0 if up else 17, points],
            send_sem=hs.at[n, g, up, k],
            recv_sem=hr.at[n, g, up, k],
            device_id={"wind": wi + 1 if up else wi - 1, "state": si},
            device_id_type=MESH,
        )

    def wind_relay(n, g, up, k):
        return pltpu.make_async_remote_copy(
            src_ref=u.at[n, g, 16 if up else 1, pl.ds(1 + 4 * k, 4)],
            dst_ref=held.at[2 * n + g, k - 1],
            send_sem=hs.at[n, g, up, k],
            recv_sem=rl.at[2 * n + g, k - 1],
            device_id={"wind": wi + 2 if up else wi - 2, "state": si},
            device_id_type=MESH,
        )

    def wind_forward(n, g, up, k):
        return pltpu.make_async_remote_copy(
            src_ref=held.at[2 * n + g, k - 1],
            dst_ref=u.at[n, g, 0 if up else 17, pl.ds(1 + 4 * k, 4)],
            send_sem=fs.at[2 * n + g, k - 1],
            recv_sem=hr.at[n, g, up, k],
            device_id={"wind": wi - 1 if up else wi + 1, "state": si},
            device_id_type=MESH,
        )

    def dens_part(up, k):
        rows = pl.ds(64 * k, 64)
        return pltpu.make_async_remote_copy(
            src_ref=d_hbm.at[15 if up else 0, rows],
            dst_ref=d.at[0 if up else 17, rows],
            send_sem=dhs.at[up, k],
            recv_sem=dhr.at[up, k],
            device_id={"wind": wi + 1 if up else wi - 1, "state": si},
            device_id_type=MESH,
        )

    def dens_relay(up, k):
        return pltpu.make_async_remote_copy(
            src_ref=d_hbm.at[15 if up else 0, pl.ds(64 * k, 64)],
            dst_ref=held_d.at[k - 1],
            send_sem=dhs.at[up, k],
            recv_sem=rl.at[2 * ITERS, k - 1],
            device_id={"wind": wi + 2 if up else wi - 2, "state": si},
            device_id_type=MESH,
        )

    def dens_forward(up, k):
        return pltpu.make_async_remote_copy(
            src_ref=held_d.at[k - 1],
            dst_ref=d.at[0 if up else 17, pl.ds(64 * k, 64)],
            send_sem=fs.at[2 * ITERS, k - 1],
            recv_sem=dhr.at[up, k],
            device_id={"wind": wi - 1 if up else wi + 1, "state": si},
            device_id_type=MESH,
        )

    def both_hold(one, other):
        return jnp.logical_and(one, other)

    def has(up):
        return wi < nw - 1 if up else wi > 0

    def by_relay(up, k):
        if up:
            return both_hold(wi % 2 == 1, both_hold(wi >= 7 - 2 * k, wi <= 5))
        return both_hold(wi % 2 == 0, both_hold(wi >= 2, wi <= 2 * k))

    def relays(up, k):
        if up:
            return both_hold(wi % 2 == 1, wi >= 9 - 2 * k)
        return both_hold(wi % 2 == 0, wi <= 2 * k - 2)

    def start_plane(part, relay, up):
        @pl.when(has(up))
        def _():
            part(up, 0).start()

        for k in (1, 2, 3):

            @pl.when(by_relay(up, k))
            def _():
                relay(up, k).start()

            @pl.when(both_hold(has(up), jnp.logical_not(by_relay(up, k))))
            def _():
                part(up, k).start()

    def start_wind(n, g, up):
        start_plane(lambda up, k: wind_part(n, g, up, k), lambda up, k: wind_relay(n, g, up, k), up)

    def start_dens(up):
        start_plane(dens_part, dens_relay, up)

    def arrive_plane(part):
        for up in (0, 1):

            @pl.when(has(1 - up))
            def _():
                for k in range(4):
                    part(up, k).wait_recv()

    def drain_plane(part, onward):
        for up in (0, 1):

            @pl.when(has(up))
            def _():
                for k in range(4):
                    part(up, k).wait_send()

            for k in (1, 2, 3):

                @pl.when(relays(up, k))
                def _():
                    onward(up, k).wait_send()

    def pass_on(relay, onward):
        for k in (1, 2, 3):
            for up in (0, 1):

                @pl.when(relays(up, k))
                def _():
                    relay(up, k).wait_recv()
                    onward(up, k).start()

    def forward(n, g):
        pass_on(lambda up, k: wind_relay(n, g, up, k), lambda up, k: wind_forward(n, g, up, k))

    def forward_dens():
        pass_on(dens_relay, dens_forward)

    def state_copies(n, g):
        down = pltpu.make_async_remote_copy(
            src_ref=u.at[n, g, pl.ds(1, 16), 1],
            dst_ref=u.at[n, g, pl.ds(1, 16), 17],
            send_sem=ss.at[n, g, 0],
            recv_sem=sr.at[n, g, 0],
            device_id={"wind": wi, "state": si - 1},
            device_id_type=MESH,
        )
        up = pltpu.make_async_remote_copy(
            src_ref=u.at[n, g, pl.ds(1, 16), 16],
            dst_ref=u.at[n, g, pl.ds(1, 16), 0],
            send_sem=ss.at[n, g, 1],
            recv_sem=sr.at[n, g, 1],
            device_id={"wind": wi, "state": si + 1},
            device_id_type=MESH,
        )
        return down, up

    def dens_state_copies():
        down = pltpu.make_async_remote_copy(
            src_ref=dks.at[0],
            dst_ref=dkr.at[1],
            send_sem=dss.at[0],
            recv_sem=dsr.at[0],
            device_id={"wind": wi, "state": si - 1},
            device_id_type=MESH,
        )
        up = pltpu.make_async_remote_copy(
            src_ref=dks.at[1],
            dst_ref=dkr.at[0],
            send_sem=dss.at[1],
            recv_sem=dsr.at[1],
            device_id={"wind": wi, "state": si + 1},
            device_id_type=MESH,
        )
        return down, up

    def start(pair, index, last):
        @pl.when(index > 0)
        def _():
            pair[0].start()

        @pl.when(index < last)
        def _():
            pair[1].start()

    def arrive(pair, index, last):
        @pl.when(index < last)
        def _():
            pair[0].wait_recv()

        @pl.when(index > 0)
        def _():
            pair[1].wait_recv()

    def drain(pair, index, last):
        @pl.when(index > 0)
        def _():
            pair[0].wait_send()

        @pl.when(index < last)
        def _():
            pair[1].wait_send()

    start_dens(0)
    start_dens(1)

    def tile_rows(g, s, kh):
        return pl.ds(g * 256 + (s // 8) * 16 + kh * 8 + s % 8, 8, stride=32)

    load_v.wait()
    for g in range(2):

        @pl.loop(0, 16)
        def _(w):
            for s in range(16):
                for kh in range(2):
                    u[0, g, w + 1, s + 1, :, halves[kh]] = vo[w, tile_rows(g, s, kh), :]

        start_wind(0, g, 0)
        start_wind(0, g, 1)
        start(state_copies(0, g), si, ns - 1)

    load_d.wait()

    @pl.loop(0, 16)
    def _(w):
        for r in range(16):
            dks[0, w, pl.ds(r, 1), :] = d[w + 1, pl.ds(r * 16, 1), :]
            dks[1, w, pl.ds(r, 1), :] = d[w + 1, pl.ds(r * 16 + 15, 1), :]

    for load in small:
        load.wait()
    row = lax.broadcasted_iota(jnp.int32, (8, 128), 0)

    @pl.loop(0, 16)
    def _(w):
        for g in range(2):
            p = jnp.zeros((8, 128), F32)
            q = jnp.zeros((8, 128), F32)
            for r in range(8):
                p = jnp.where(row == r, price_s[w, g * 8 + r], p)
                q = jnp.where(row == r, rate_s[w, g * 8 + r], q)
            pb[g, w] = 0.5 * p
            qb[g, w] = step_size * q

    group = lax.broadcasted_iota(jnp.int32, (8, 128), 1) // 16
    for g in range(2):
        for h in range(2):
            rb[g, h, pl.ds(0, 8), :] = jnp.zeros((8, 128), F32)
            rb[g, h, pl.ds(2056, 8), :] = jnp.zeros((8, 128), F32)

            @pl.loop(0, 8)
            def _(r):
                p = jnp.zeros((1, 128), F32)
                for w in range(8):
                    p = jnp.where(group[:1] == w, 0.5 * price_s[h * 8 + w, g * 8 + r], p)
                pc[g, h, pl.ds(r, 1), :] = p

    for i, out in enumerate((rt, rs)):
        hi, lo = split(inv[i].T)
        out[pl.ds(0, 256)] = hi
        out[pl.ds(256, 256)] = lo

    def matmul(r):
        return (
            jnp.dot(x[:, pl.ds(0, 256)], r[pl.ds(0, 256)], preferred_element_type=F32)
            + jnp.dot(x[:, pl.ds(256, 256)], r[pl.ds(0, 256)], preferred_element_type=F32)
            + jnp.dot(x[:, pl.ds(0, 256)], r[pl.ds(256, 256)], preferred_element_type=F32)
        )

    def both(tile):
        return jnp.concatenate([tile, tile], axis=1)[None]

    def own_copy(g, h):
        return pltpu.make_async_copy(
            sb.at[g, h, si], rb.at[g, h, pl.ds(pl.multiple_of(8 + si * 128, 8), 128)], own_sem.at[g, h]
        )

    def regroup(g, h):
        @pl.loop(0, 4)
        def _(quad):
            for i in range(4):
                s = quad * 4 + i
                for kh in range(2):
                    a = [uf[g, h * 8 + w, s, :, halves[kh]] for w in range(8)]
                    for bit in (4, 2, 1):
                        high = (group // bit) % 2 == 1
                        b = [None] * 8
                        for w in range(8):
                            if w & bit == 0:
                                b[w] = jnp.where(high, pltpu.roll(a[w + bit], 16 * bit, 1), a[w])
                                b[w + bit] = jnp.where(high, a[w + bit], pltpu.roll(a[w], 128 - 16 * bit, 1))
                        a = b
                    for w in range(8):
                        sb[g, h, kh * 8 + w, pl.ds(pl.multiple_of(s * 8, 8), 8), :] = a[w]

    def send(g, h):
        own_copy(g, h).start()

        @pl.loop(1, ns)
        def _(p):
            q = (3 * p) % ns
            to = (si // 4 + q // 4) % 4 * 4 + (si // 2 + q // 2) % 2 * 2 + (si + q) % 2
            pltpu.make_async_remote_copy(
                src_ref=sb.at[g, h, to],
                dst_ref=rb.at[g, h, pl.ds(pl.multiple_of(8 + si * 128, 8), 128)],
                send_sem=as_sem.at[g, h],
                recv_sem=ar_sem.at[g, h],
                device_id={"wind": wi, "state": to},
                device_id_type=MESH,
            ).start()

    forward(0, 0)

    @pl.loop(0, 2 * ITERS)
    def _(m):
        n = m // 2
        g = m % 2
        arrive_plane(lambda up, k: wind_part(n, g, up, k))
        arrive(state_copies(n, g), si, ns - 1)

        @pl.when(m < 2 * ITERS - 1)
        def _():
            forward((m + 1) // 2, (m + 1) % 2)

        @pl.when(m == 1)
        def _():
            forward_dens()

        @pl.when(m == 2 * ITERS - 1)
        def _():
            for h in range(2):
                send(0, h)


        @pl.loop(0, 4)
        def _(turn):
            c = (turn * 3) % 4

            @pl.loop(0, 4)
            def _(j):
                w = c * 4 + j
                half = 0.25 * (u[n, g, w + 1, pl.ds(2, 16)] - u[n, g, w + 1, pl.ds(0, 16)]) + both(pb[g, w])
                t = jnp.tanh(half)
                mid = u[n, g, w + 1, pl.ds(1, 16)]
                couple = u[n, g, w + 2, pl.ds(1, 16)] + u[n, g, w, pl.ds(1, 16)] - 2.0 * mid
                source = (
                    u[0, g, w + 1, pl.ds(1, 16)] + 0.5 * t * (t - 2.0 * half) + both(qb[g, w]) * couple
                )
                hi, lo = split(source.reshape(128, 256))
                rows = pl.ds(pl.multiple_of(j * 128, 128), 128)
                x[rows, pl.ds(0, 256)] = hi
                x[rows, pl.ds(256, 256)] = lo

            swept = matmul(rt).reshape(4, 16, 8, 256)

            @pl.when(n < ITERS - 1)
            def _():
                u[n + 1, g, pl.ds(c * 4 + 1, 4), pl.ds(1, 16)] = swept

                @pl.when(turn == 0)
                def _():
                    start_wind(n + 1, g, 0)

                @pl.when(turn == 1)
                def _():
                    start_wind(n + 1, g, 1)

            @pl.when(n == ITERS - 1)
            def _():
                uf[g, pl.ds(c * 4, 4)] = swept

        @pl.when(n < ITERS - 1)
        def _():
            start(state_copies(n + 1, g), si, ns - 1)

        @pl.when(m == 1)
        def _():
            start(dens_state_copies(), si, ns - 1)

        @pl.when(n == ITERS - 1)
        def _():
            for h in range(2):
                regroup(g, h)

            @pl.when(g == 1)
            def _():
                for h in range(2):
                    send(1, h)

    @pl.loop(0, 16)
    def _(w):
        for g in range(2):
            for s in range(16):
                for kh in range(2):
                    vo[w, tile_rows(g, s, kh), :] = uf[g, w, s, :, halves[kh]]

    arrive_plane(dens_part)
    arrive(dens_state_copies(), si, ns - 1)
    level = lax.broadcasted_iota(jnp.int32, (16, 256), 0)

    @pl.loop(0, 16)
    def _(w):
        @pl.loop(0, 16)
        def _(r):
            rows = pl.ds(pl.multiple_of(r * 16, 16), 16)
            mid = d[w + 1, rows, :]
            above = jnp.where(level == 15, dkr[1, w, pl.ds(r, 1), :], pltpu.roll(mid, 15, 0))
            below = jnp.where(level == 0, dkr[0, w, pl.ds(r, 1), :], pltpu.roll(mid, 1, 0))
            couple = d[w + 2, rows, :] + d[w, rows, :] - 2.0 * mid
            source = (
                mid
                + (step_size * tank_spread) * (above + below - 2.0 * mid)
                + (step_size * rate_s[w, r]) * couple
            )
            for kh in range(2):
                do[w, pl.ds(r * 2, 2), kh] = source[:, kh * 128 : (kh + 1) * 128].reshape(2, 8, 128)

    point = lax.broadcasted_iota(jnp.int32, (128, 256), 1)

    def all_blocks(g, h, sem):
        blocks = sb.at[g, h, pl.ds(0, ns - 1)]
        return pltpu.make_async_copy(blocks, blocks, sem.at[g, h])

    @pl.loop(0, 4)
    def _(m):
        g = m // 2
        h = m % 2
        own_copy(g, h).wait()
        all_blocks(g, h, ar_sem).wait()

        @pl.loop(0, 2)
        def _(c):
            @pl.loop(0, 4, unroll=4)
            def _(j):
                r = c * 4 + j
                rows = pl.ds(pl.multiple_of((g * 8 + r) * 16, 16), 16)
                tiles = pl.ds((g * 8 + r) * 2, 2)
                above = rb[g, h, pl.ds(r + 16, 256, stride=8), :]
                below = rb[g, h, pl.ds(r, 256, stride=8), :]
                drift = (-2.0 * jnp.tanh(0.25 * (above - below) + pc[g, h, pl.ds(r, 1), :])).T
                flux = drift * d[pl.ds(1 + h * 8, 8), rows, :].reshape(128, 256)
                upper = jnp.where(point == 255, 0.0, pltpu.roll(flux, 255, 1))
                lower = jnp.where(point == 0, 0.0, pltpu.roll(flux, 1, 1))
                still = jnp.concatenate(
                    [do[pl.ds(h * 8, 8), tiles, kh].reshape(128, 128) for kh in range(2)], axis=1
                )
                source = still - (0.5 * step_size) * (upper - lower)
                hi, lo = split(source)
                at = pl.ds(pl.multiple_of(j * 128, 128), 128)
                x[at, pl.ds(0, 256)] = hi
                x[at, pl.ds(256, 256)] = lo

            out = matmul(rs)
            for j in range(4):
                tiles = pl.ds((g * 8 + c * 4 + j) * 2, 2)
                for kh in range(2):
                    do[pl.ds(h * 8, 8), tiles, kh] = out[
                        j * 128 : (j + 1) * 128, kh * 128 : (kh + 1) * 128
                    ].reshape(8, 2, 8, 128)

    @pl.loop(0, 4)
    def _(m):
        g = m // 2
        h = m % 2
        all_blocks(g, h, as_sem).wait()

    @pl.loop(0, 2 * ITERS)
    def _(m):
        n = m // 2
        g = m % 2
        drain_plane(lambda up, k: wind_part(n, g, up, k), lambda up, k: wind_forward(n, g, up, k))
        drain(state_copies(n, g), si, ns - 1)

    drain_plane(dens_part, dens_forward)
    drain(dens_state_copies(), si, ns - 1)


def on_device(value_next, density, price, wind_rate, tank_inverse, soc_inverse):
    vmem = pl.BlockSpec(memory_space=pltpu.VMEM)
    hbm = pl.BlockSpec(memory_space=pltpu.HBM)
    dma = pltpu.SemaphoreType.DMA
    tiles = value_next.reshape(16, 32, 8, 2, 128).transpose(0, 1, 3, 2, 4).reshape(16, 512, 128)
    value, dens = pl.pallas_call(
        body,
        name="storage_step",
        out_shape=(
            jax.ShapeDtypeStruct((16, 512, 128), F32),
            jax.ShapeDtypeStruct((16, 32, 2, 8, 128), F32),
        ),
        in_specs=[hbm] * 6,
        out_specs=(vmem, vmem),
        scratch_shapes=[
            pltpu.VMEM((ITERS, 2, 18, 18, 8, 256), F32),
            pltpu.VMEM((2, 16, 16, 8, 256), F32),
            pltpu.VMEM((512, 512), BF16),
            pltpu.VMEM((512, 256), BF16),
            pltpu.VMEM((512, 256), BF16),
            pltpu.VMEM((2, 16, 8, 128), F32),
            pltpu.VMEM((2, 16, 8, 128), F32),
            pltpu.VMEM((18, 256, 256), F32),
            pltpu.VMEM((2, 16, 16, 256), F32),
            pltpu.VMEM((2, 16, 16, 256), F32),
            pltpu.VMEM((2, 2, 8, 128), F32),
            pltpu.VMEM((2, 2, 16, 128, 128), F32),
            pltpu.VMEM((2, 2, 2064, 128), F32),
            pltpu.SMEM((16, 16), F32),
            pltpu.SMEM((16, 16), F32),
            pltpu.VMEM((2, 256, 256), F32),
            pltpu.VMEM((2 * ITERS, 3, 4, 8, 256), F32),
            pltpu.VMEM((3, 64, 256), F32),
            dma((6,)),
            dma((ITERS, 2, 2, 4)),
            dma((ITERS, 2, 2, 4)),
            dma((ITERS, 2, 2)),
            dma((ITERS, 2, 2)),
            dma((2, 4)),
            dma((2, 4)),
            dma((2,)),
            dma((2,)),
            dma((2, 2)),
            dma((2, 2)),
            dma((2, 2)),
            dma((2 * ITERS + 1, 3)),
            dma((2 * ITERS + 1, 3)),
        ],
        compiler_params=pltpu.CompilerParams(
            collective_id=0, has_side_effects=True, vmem_limit_bytes=42 * 1024 * 1024
        ),
    )(*[pltpu.with_memory_space_constraint(a, pltpu.HBM) for a in (price, wind_rate, tank_inverse, soc_inverse, tiles, density.reshape(16, 256, 256))])

    def whole(out):
        return out.reshape(16, 32, 2, 8, 128).transpose(0, 1, 3, 2, 4).reshape(16, 16, 16, 256)

    return whole(value), whole(dens)


def solution(mesh):
    placed = (
        P("wind", None, "state", None),
        P("wind", None, "state", None),
        P("wind", None),
        P("wind", None),
        P(),
        P(),
    )
    return jax.shard_map(
        on_device,
        mesh=mesh,
        in_specs=placed,
        out_specs=(P("wind", None, "state", None), P("wind", None, "state", None)),
        check_vma=False,
    )
```

```python
import jax
import jax.numpy as jnp
from jax import lax
from jax.experimental import pallas as pl
from jax.experimental.pallas import tpu as pltpu
from jax.sharding import PartitionSpec as P

ITERS = 4
MESH = pl.DeviceIdType.MESH

step_size = 0.25
tank_spread = 0.3

F32 = jnp.float32
BF16 = jnp.bfloat16


def split(x):
    hi = x.astype(BF16)
    lo = (x - hi.astype(F32)).astype(BF16)
    return hi, lo


def product(x, r):
    return (
        jnp.dot(x[:, pl.ds(0, 256)], r[pl.ds(0, 256)], preferred_element_type=F32)
        + jnp.dot(x[:, pl.ds(256, 256)], r[pl.ds(0, 256)], preferred_element_type=F32)
        + jnp.dot(x[:, pl.ds(0, 256)], r[pl.ds(256, 256)], preferred_element_type=F32)
    )


def density_part(g, h, x, rs, d, pc, rb, still_ref, out_ref):
    point = lax.broadcasted_iota(jnp.int32, (128, 256), 1)
    winds = pl.ds(h * 8, 8)

    @pl.loop(0, 2)
    def _(c):
        @pl.loop(0, 4, unroll=4)
        def _(j):
            r = c * 4 + j
            rows = pl.ds(pl.multiple_of((g * 8 + r) * 16, 16), 16)
            tiles = pl.ds((g * 8 + r) * 2, 2)
            above = rb[g, h, pl.ds(r + 16, 256, stride=8), :]
            below = rb[g, h, pl.ds(r, 256, stride=8), :]
            drift = (-2.0 * jnp.tanh(0.25 * (above - below) + pc[g, h, pl.ds(r, 1), :])).T
            flux = drift * d[pl.ds(1 + h * 8, 8), rows, :].reshape(128, 256)
            upper = jnp.where(point == 255, 0.0, pltpu.roll(flux, 255, 1))
            lower = jnp.where(point == 0, 0.0, pltpu.roll(flux, 1, 1))
            still = jnp.concatenate(
                [still_ref[winds, tiles, kh].reshape(128, 128) for kh in range(2)], axis=1
            )
            hi, lo = split(still - (0.5 * step_size) * (upper - lower))
            at = pl.ds(pl.multiple_of(j * 128, 128), 128)
            x[at, pl.ds(0, 256)] = hi
            x[at, pl.ds(256, 256)] = lo

        out = product(x, rs)
        for j in range(4):
            for kh in range(2):
                out_ref[:, pl.ds((c * 4 + j) * 2, 2), kh] = out[
                    j * 128 : (j + 1) * 128, kh * 128 : (kh + 1) * 128
                ].reshape(8, 2, 8, 128)


def body(
    price_hbm,
    rate_hbm,
    tinv_hbm,
    sinv_hbm,
    v_hbm,
    d_hbm,
    vo,
    do,
    rs,
    d,
    pc,
    rb,
    u,
    uf,
    x,
    rt,
    pb,
    qb,
    dks,
    dkr,
    sb,
    price_s,
    rate_s,
    inv,
    held,
    held_d,
    ld_sem,
    hs,
    hr,
    ss,
    sr,
    dhs,
    dhr,
    dss,
    dsr,
    as_sem,
    ar_sem,
    own_sem,
    rl,
    fs,
):
    wi = lax.axis_index("wind")
    si = lax.axis_index("state")
    nw = 8
    ns = 16

    halves = (pl.ds(0, 128), pl.ds(128, 128))
    load_v = pltpu.make_async_copy(v_hbm, vo, ld_sem.at[0])
    load_d = pltpu.make_async_copy(d_hbm, d.at[pl.ds(1, 16)], ld_sem.at[1])
    load_v.start()
    load_d.start()
    small = [
        pltpu.make_async_copy(src, dst, ld_sem.at[2 + i])
        for i, (src, dst) in enumerate(
            ((price_hbm, price_s), (rate_hbm, rate_s), (tinv_hbm, inv.at[0]), (sinv_hbm, inv.at[1]))
        )
    ]
    for load in small:
        load.start()

    barrier = pltpu.get_barrier_semaphore()

    @pl.loop(1, ns)
    def _(p):
        pl.semaphore_signal(
            barrier, inc=1, device_id={"wind": wi, "state": (si + p) % ns}, device_id_type=MESH
        )

    @pl.when(wi > 0)
    def _():
        pl.semaphore_signal(barrier, inc=1, device_id={"wind": wi - 1, "state": si}, device_id_type=MESH)

    @pl.when(wi < nw - 1)
    def _():
        pl.semaphore_signal(barrier, inc=1, device_id={"wind": wi + 1, "state": si}, device_id_type=MESH)

    @pl.when(wi == 0)
    def _():
        d[0] = jnp.zeros((256, 256), F32)

        @pl.loop(0, ITERS)
        def _(n):
            for g in range(2):
                u[n, g, 0] = jnp.zeros((18, 8, 256), F32)

    @pl.when(wi == nw - 1)
    def _():
        d[17] = jnp.zeros((256, 256), F32)

        @pl.loop(0, ITERS)
        def _(n):
            for g in range(2):
                u[n, g, 17] = jnp.zeros((18, 8, 256), F32)

    @pl.when(si == 0)
    def _():
        dkr[0] = jnp.zeros((16, 16, 256), F32)

        @pl.loop(0, ITERS)
        def _(n):
            for g in range(2):
                u[n, g, pl.ds(1, 16), 0] = jnp.zeros((16, 8, 256), F32)

    @pl.when(si == ns - 1)
    def _():
        dkr[1] = jnp.zeros((16, 16, 256), F32)

        @pl.loop(0, ITERS)
        def _(n):
            for g in range(2):
                u[n, g, pl.ds(1, 16), 17] = jnp.zeros((16, 8, 256), F32)

    @pl.when(wi >= 2)
    def _():
        pl.semaphore_signal(barrier, inc=1, device_id={"wind": wi - 2, "state": si}, device_id_type=MESH)

    @pl.when(wi < nw - 2)
    def _():
        pl.semaphore_signal(barrier, inc=1, device_id={"wind": wi + 2, "state": si}, device_id_type=MESH)

    expected = ns - 1
    for near in (wi > 0, wi < nw - 1, wi >= 2, wi < nw - 2):
        expected = expected + jnp.where(near, 1, 0)
    pl.semaphore_wait(barrier, expected)

    def wind_part(n, g, up, k):
        points = pl.ds(1 + 4 * k, 4)
        return pltpu.make_async_remote_copy(
            src_ref=u.at[n, g, 16 if up else 1, points],
            dst_ref=u.at[n, g, 0 if up else 17, points],
            send_sem=hs.at[n, g, up, k],
            recv_sem=hr.at[n, g, up, k],
            device_id={"wind": wi + 1 if up else wi - 1, "state": si},
            device_id_type=MESH,
        )

    def wind_relay(n, g, up, k):
        return pltpu.make_async_remote_copy(
            src_ref=u.at[n, g, 16 if up else 1, pl.ds(1 + 4 * k, 4)],
            dst_ref=held.at[2 * n + g, k - 1],
            send_sem=hs.at[n, g, up, k],
            recv_sem=rl.at[2 * n + g, k - 1],
            device_id={"wind": wi + 2 if up else wi - 2, "state": si},
            device_id_type=MESH,
        )

    def wind_forward(n, g, up, k):
        return pltpu.make_async_remote_copy(
            src_ref=held.at[2 * n + g, k - 1],
            dst_ref=u.at[n, g, 0 if up else 17, pl.ds(1 + 4 * k, 4)],
            send_sem=fs.at[2 * n + g, k - 1],
            recv_sem=hr.at[n, g, up, k],
            device_id={"wind": wi - 1 if up else wi + 1, "state": si},
            device_id_type=MESH,
        )

    def dens_part(up, k):
        rows = pl.ds(64 * k, 64)
        return pltpu.make_async_remote_copy(
            src_ref=d_hbm.at[15 if up else 0, rows],
            dst_ref=d.at[0 if up else 17, rows],
            send_sem=dhs.at[up, k],
            recv_sem=dhr.at[up, k],
            device_id={"wind": wi + 1 if up else wi - 1, "state": si},
            device_id_type=MESH,
        )

    def dens_relay(up, k):
        return pltpu.make_async_remote_copy(
            src_ref=d_hbm.at[15 if up else 0, pl.ds(64 * k, 64)],
            dst_ref=held_d.at[k - 1],
            send_sem=dhs.at[up, k],
            recv_sem=rl.at[2 * ITERS, k - 1],
            device_id={"wind": wi + 2 if up else wi - 2, "state": si},
            device_id_type=MESH,
        )

    def dens_forward(up, k):
        return pltpu.make_async_remote_copy(
            src_ref=held_d.at[k - 1],
            dst_ref=d.at[0 if up else 17, pl.ds(64 * k, 64)],
            send_sem=fs.at[2 * ITERS, k - 1],
            recv_sem=dhr.at[up, k],
            device_id={"wind": wi - 1 if up else wi + 1, "state": si},
            device_id_type=MESH,
        )

    def both_hold(one, other):
        return jnp.logical_and(one, other)

    def has(up):
        return wi < nw - 1 if up else wi > 0

    def by_relay(up, k):
        if up:
            return both_hold(wi % 2 == 1, both_hold(wi >= 7 - 2 * k, wi <= 5))
        return both_hold(wi % 2 == 0, both_hold(wi >= 2, wi <= 2 * k))

    def relays(up, k):
        if up:
            return both_hold(wi % 2 == 1, wi >= 9 - 2 * k)
        return both_hold(wi % 2 == 0, wi <= 2 * k - 2)

    def start_plane(part, relay, up):
        @pl.when(has(up))
        def _():
            part(up, 0).start()

        for k in (1, 2, 3):

            @pl.when(by_relay(up, k))
            def _():
                relay(up, k).start()

            @pl.when(both_hold(has(up), jnp.logical_not(by_relay(up, k))))
            def _():
                part(up, k).start()

    def start_wind(n, g, up):
        start_plane(lambda up, k: wind_part(n, g, up, k), lambda up, k: wind_relay(n, g, up, k), up)

    def start_dens(up):
        start_plane(dens_part, dens_relay, up)

    def arrive_plane(part):
        for up in (0, 1):

            @pl.when(has(1 - up))
            def _():
                for k in range(4):
                    part(up, k).wait_recv()

    def drain_plane(part, onward):
        for up in (0, 1):

            @pl.when(has(up))
            def _():
                for k in range(4):
                    part(up, k).wait_send()

            for k in (1, 2, 3):

                @pl.when(relays(up, k))
                def _():
                    onward(up, k).wait_send()

    def pass_on(relay, onward):
        for k in (1, 2, 3):
            for up in (0, 1):

                @pl.when(relays(up, k))
                def _():
                    relay(up, k).wait_recv()
                    onward(up, k).start()

    def forward(n, g):
        pass_on(lambda up, k: wind_relay(n, g, up, k), lambda up, k: wind_forward(n, g, up, k))

    def forward_dens():
        pass_on(dens_relay, dens_forward)

    def state_copies(n, g):
        down = pltpu.make_async_remote_copy(
            src_ref=u.at[n, g, pl.ds(1, 16), 1],
            dst_ref=u.at[n, g, pl.ds(1, 16), 17],
            send_sem=ss.at[n, g, 0],
            recv_sem=sr.at[n, g, 0],
            device_id={"wind": wi, "state": si - 1},
            device_id_type=MESH,
        )
        up = pltpu.make_async_remote_copy(
            src_ref=u.at[n, g, pl.ds(1, 16), 16],
            dst_ref=u.at[n, g, pl.ds(1, 16), 0],
            send_sem=ss.at[n, g, 1],
            recv_sem=sr.at[n, g, 1],
            device_id={"wind": wi, "state": si + 1},
            device_id_type=MESH,
        )
        return down, up

    def dens_state_copies():
        down = pltpu.make_async_remote_copy(
            src_ref=dks.at[0],
            dst_ref=dkr.at[1],
            send_sem=dss.at[0],
            recv_sem=dsr.at[0],
            device_id={"wind": wi, "state": si - 1},
            device_id_type=MESH,
        )
        up = pltpu.make_async_remote_copy(
            src_ref=dks.at[1],
            dst_ref=dkr.at[0],
            send_sem=dss.at[1],
            recv_sem=dsr.at[1],
            device_id={"wind": wi, "state": si + 1},
            device_id_type=MESH,
        )
        return down, up

    def start(pair, index, last):
        @pl.when(index > 0)
        def _():
            pair[0].start()

        @pl.when(index < last)
        def _():
            pair[1].start()

    def arrive(pair, index, last):
        @pl.when(index < last)
        def _():
            pair[0].wait_recv()

        @pl.when(index > 0)
        def _():
            pair[1].wait_recv()

    def drain(pair, index, last):
        @pl.when(index > 0)
        def _():
            pair[0].wait_send()

        @pl.when(index < last)
        def _():
            pair[1].wait_send()

    start_dens(0)
    start_dens(1)

    def tile_rows(g, s, kh):
        return pl.ds(g * 256 + (s // 8) * 16 + kh * 8 + s % 8, 8, stride=32)

    load_v.wait()
    for g in range(2):

        @pl.loop(0, 16)
        def _(w):
            for s in range(16):
                for kh in range(2):
                    u[0, g, w + 1, s + 1, :, halves[kh]] = vo[w, tile_rows(g, s, kh), :]

        start_wind(0, g, 0)
        start_wind(0, g, 1)
        start(state_copies(0, g), si, ns - 1)

    load_d.wait()

    @pl.loop(0, 16)
    def _(w):
        for r in range(16):
            dks[0, w, pl.ds(r, 1), :] = d[w + 1, pl.ds(r * 16, 1), :]
            dks[1, w, pl.ds(r, 1), :] = d[w + 1, pl.ds(r * 16 + 15, 1), :]

    for load in small:
        load.wait()
    row = lax.broadcasted_iota(jnp.int32, (8, 128), 0)

    @pl.loop(0, 16)
    def _(w):
        for g in range(2):
            p = jnp.zeros((8, 128), F32)
            q = jnp.zeros((8, 128), F32)
            for r in range(8):
                p = jnp.where(row == r, price_s[w, g * 8 + r], p)
                q = jnp.where(row == r, rate_s[w, g * 8 + r], q)
            pb[g, w] = 0.5 * p
            qb[g, w] = step_size * q

    group = lax.broadcasted_iota(jnp.int32, (8, 128), 1) // 16
    for g in range(2):
        for h in range(2):
            rb[g, h, pl.ds(0, 8), :] = jnp.zeros((8, 128), F32)
            rb[g, h, pl.ds(2056, 8), :] = jnp.zeros((8, 128), F32)

            @pl.loop(0, 8)
            def _(r):
                p = jnp.zeros((1, 128), F32)
                for w in range(8):
                    p = jnp.where(group[:1] == w, 0.5 * price_s[h * 8 + w, g * 8 + r], p)
                pc[g, h, pl.ds(r, 1), :] = p

    for i, out in enumerate((rt, rs)):
        hi, lo = split(inv[i].T)
        out[pl.ds(0, 256)] = hi
        out[pl.ds(256, 256)] = lo

    def both(tile):
        return jnp.concatenate([tile, tile], axis=1)[None]

    def own_copy(g, h):
        return pltpu.make_async_copy(
            sb.at[g, h, si], rb.at[g, h, pl.ds(pl.multiple_of(8 + si * 128, 8), 128)], own_sem.at[g, h]
        )

    def regroup(g, h):
        @pl.loop(0, 4)
        def _(quad):
            for i in range(4):
                s = quad * 4 + i
                for kh in range(2):
                    a = [uf[g, h * 8 + w, s, :, halves[kh]] for w in range(8)]
                    for bit in (4, 2, 1):
                        high = (group // bit) % 2 == 1
                        b = [None] * 8
                        for w in range(8):
                            if w & bit == 0:
                                b[w] = jnp.where(high, pltpu.roll(a[w + bit], 16 * bit, 1), a[w])
                                b[w + bit] = jnp.where(high, a[w + bit], pltpu.roll(a[w], 128 - 16 * bit, 1))
                        a = b
                    for w in range(8):
                        sb[g, h, kh * 8 + w, pl.ds(pl.multiple_of(s * 8, 8), 8), :] = a[w]

    def send(g, h):
        own_copy(g, h).start()

        @pl.loop(1, ns)
        def _(p):
            q = (3 * p) % ns
            to = (si // 4 + q // 4) % 4 * 4 + (si // 2 + q // 2) % 2 * 2 + (si + q) % 2
            pltpu.make_async_remote_copy(
                src_ref=sb.at[g, h, to],
                dst_ref=rb.at[g, h, pl.ds(pl.multiple_of(8 + si * 128, 8), 128)],
                send_sem=as_sem.at[g, h],
                recv_sem=ar_sem.at[g, h],
                device_id={"wind": wi, "state": to},
                device_id_type=MESH,
            ).start()

    forward(0, 0)

    @pl.loop(0, 2 * ITERS)
    def _(m):
        n = m // 2
        g = m % 2
        arrive_plane(lambda up, k: wind_part(n, g, up, k))
        arrive(state_copies(n, g), si, ns - 1)

        @pl.when(m < 2 * ITERS - 1)
        def _():
            forward((m + 1) // 2, (m + 1) % 2)

        @pl.when(m == 1)
        def _():
            forward_dens()

        @pl.when(m == 2 * ITERS - 1)
        def _():
            for h in range(2):
                send(0, h)


        @pl.loop(0, 4)
        def _(turn):
            c = (turn * 3) % 4

            @pl.loop(0, 4)
            def _(j):
                w = c * 4 + j
                half = 0.25 * (u[n, g, w + 1, pl.ds(2, 16)] - u[n, g, w + 1, pl.ds(0, 16)]) + both(pb[g, w])
                t = jnp.tanh(half)
                mid = u[n, g, w + 1, pl.ds(1, 16)]
                couple = u[n, g, w + 2, pl.ds(1, 16)] + u[n, g, w, pl.ds(1, 16)] - 2.0 * mid
                source = (
                    u[0, g, w + 1, pl.ds(1, 16)] + 0.5 * t * (t - 2.0 * half) + both(qb[g, w]) * couple
                )
                hi, lo = split(source.reshape(128, 256))
                rows = pl.ds(pl.multiple_of(j * 128, 128), 128)
                x[rows, pl.ds(0, 256)] = hi
                x[rows, pl.ds(256, 256)] = lo

            swept = product(x, rt).reshape(4, 16, 8, 256)

            @pl.when(n < ITERS - 1)
            def _():
                u[n + 1, g, pl.ds(c * 4 + 1, 4), pl.ds(1, 16)] = swept

                @pl.when(turn == 0)
                def _():
                    start_wind(n + 1, g, 0)

                @pl.when(turn == 1)
                def _():
                    start_wind(n + 1, g, 1)

            @pl.when(n == ITERS - 1)
            def _():
                uf[g, pl.ds(c * 4, 4)] = swept

        @pl.when(n < ITERS - 1)
        def _():
            start(state_copies(n + 1, g), si, ns - 1)

        @pl.when(m == 1)
        def _():
            start(dens_state_copies(), si, ns - 1)

        @pl.when(n == ITERS - 1)
        def _():
            for h in range(2):
                regroup(g, h)

            @pl.when(g == 1)
            def _():
                for h in range(2):
                    send(1, h)

    @pl.loop(0, 16)
    def _(w):
        for g in range(2):
            for s in range(16):
                for kh in range(2):
                    vo[w, tile_rows(g, s, kh), :] = uf[g, w, s, :, halves[kh]]

    arrive_plane(dens_part)
    arrive(dens_state_copies(), si, ns - 1)
    level = lax.broadcasted_iota(jnp.int32, (16, 256), 0)

    @pl.loop(0, 16)
    def _(w):
        @pl.loop(0, 16)
        def _(r):
            rows = pl.ds(pl.multiple_of(r * 16, 16), 16)
            mid = d[w + 1, rows, :]
            above = jnp.where(level == 15, dkr[1, w, pl.ds(r, 1), :], pltpu.roll(mid, 15, 0))
            below = jnp.where(level == 0, dkr[0, w, pl.ds(r, 1), :], pltpu.roll(mid, 1, 0))
            couple = d[w + 2, rows, :] + d[w, rows, :] - 2.0 * mid
            source = (
                mid
                + (step_size * tank_spread) * (above + below - 2.0 * mid)
                + (step_size * rate_s[w, r]) * couple
            )
            for kh in range(2):
                do[w, pl.ds(r * 2, 2), kh] = source[:, kh * 128 : (kh + 1) * 128].reshape(2, 8, 128)

    def all_blocks(g, h, sem):
        blocks = sb.at[g, h, pl.ds(0, ns - 1)]
        return pltpu.make_async_copy(blocks, blocks, sem.at[g, h])

    @pl.loop(0, 4)
    def _(m):
        g = m // 2
        h = m % 2
        own_copy(g, h).wait()
        all_blocks(g, h, ar_sem).wait()

        @pl.when(m < 3)
        def _():
            density_part(g, h, x, rs, d, pc, rb, do, do.at[pl.ds(h * 8, 8), pl.ds(g * 16, 16)])

    @pl.loop(0, 4)
    def _(m):
        g = m // 2
        h = m % 2
        all_blocks(g, h, as_sem).wait()

    @pl.loop(0, 2 * ITERS)
    def _(m):
        n = m // 2
        g = m % 2
        drain_plane(lambda up, k: wind_part(n, g, up, k), lambda up, k: wind_forward(n, g, up, k))
        drain(state_copies(n, g), si, ns - 1)

    drain_plane(dens_part, dens_forward)
    drain(dens_state_copies(), si, ns - 1)


def finish(value_ref, still_ref, rs, d, pc, rb, value_hbm, dens_hbm, x, last, sem):
    copies = [
        pltpu.make_async_copy(value_ref.at[pl.ds(i * 4, 4)], value_hbm.at[pl.ds(i * 4, 4)], sem.at[i])
        for i in range(4)
    ]
    for i, (winds, tiles) in enumerate(
        ((pl.ds(0, 8), pl.ds(0, 16)), (pl.ds(8, 8), pl.ds(0, 16)), (pl.ds(0, 8), pl.ds(16, 16)))
    ):
        copies.append(
            pltpu.make_async_copy(still_ref.at[winds, tiles], dens_hbm.at[winds, tiles], sem.at[4 + i])
        )
    for copy in copies:
        copy.start()
    density_part(1, 1, x, rs, d, pc, rb, still_ref, last)
    ending = pltpu.make_async_copy(last, dens_hbm.at[pl.ds(8, 8), pl.ds(16, 16)], sem.at[7])
    ending.start()
    for copy in copies:
        copy.wait()
    ending.wait()


def on_device(value_next, density, price, wind_rate, tank_inverse, soc_inverse):
    vmem = pl.BlockSpec(memory_space=pltpu.VMEM)
    hbm = pl.BlockSpec(memory_space=pltpu.HBM)
    dma = pltpu.SemaphoreType.DMA
    tiles = value_next.reshape(16, 32, 8, 2, 128).transpose(0, 1, 3, 2, 4).reshape(16, 512, 128)
    value, dens, *rest = pl.pallas_call(
        body,
        name="storage_step",
        out_shape=(
            jax.ShapeDtypeStruct((16, 512, 128), F32),
            jax.ShapeDtypeStruct((16, 32, 2, 8, 128), F32),
            jax.ShapeDtypeStruct((512, 256), BF16),
            jax.ShapeDtypeStruct((18, 256, 256), F32),
            jax.ShapeDtypeStruct((2, 2, 8, 128), F32),
            jax.ShapeDtypeStruct((2, 2, 2064, 128), F32),
        ),
        in_specs=[hbm] * 6,
        out_specs=(vmem,) * 6,
        scratch_shapes=[
            pltpu.VMEM((ITERS, 2, 18, 18, 8, 256), F32),
            pltpu.VMEM((2, 16, 16, 8, 256), F32),
            pltpu.VMEM((512, 512), BF16),
            pltpu.VMEM((512, 256), BF16),
            pltpu.VMEM((2, 16, 8, 128), F32),
            pltpu.VMEM((2, 16, 8, 128), F32),
            pltpu.VMEM((2, 16, 16, 256), F32),
            pltpu.VMEM((2, 16, 16, 256), F32),
            pltpu.VMEM((2, 2, 16, 128, 128), F32),
            pltpu.SMEM((16, 16), F32),
            pltpu.SMEM((16, 16), F32),
            pltpu.VMEM((2, 256, 256), F32),
            pltpu.VMEM((2 * ITERS, 3, 4, 8, 256), F32),
            pltpu.VMEM((3, 64, 256), F32),
            dma((6,)),
            dma((ITERS, 2, 2, 4)),
            dma((ITERS, 2, 2, 4)),
            dma((ITERS, 2, 2)),
            dma((ITERS, 2, 2)),
            dma((2, 4)),
            dma((2, 4)),
            dma((2,)),
            dma((2,)),
            dma((2, 2)),
            dma((2, 2)),
            dma((2, 2)),
            dma((2 * ITERS + 1, 3)),
            dma((2 * ITERS + 1, 3)),
        ],
        compiler_params=pltpu.CompilerParams(
            collective_id=0, has_side_effects=True, vmem_limit_bytes=33 * 1024 * 1024
        ),
    )(*[pltpu.with_memory_space_constraint(a, pltpu.HBM) for a in (price, wind_rate, tank_inverse, soc_inverse, tiles, density.reshape(16, 256, 256))])

    value, dens = pl.pallas_call(
        finish,
        name="finish",
        out_shape=(
            jax.ShapeDtypeStruct((16, 512, 128), F32),
            jax.ShapeDtypeStruct((16, 32, 2, 8, 128), F32),
        ),
        in_specs=[vmem] * 6,
        out_specs=(hbm, hbm),
        scratch_shapes=[pltpu.VMEM((512, 512), BF16), pltpu.VMEM((8, 16, 2, 8, 128), F32), dma((8,))],
        compiler_params=pltpu.CompilerParams(vmem_limit_bytes=8 * 1024 * 1024),
    )(value, dens, *rest)

    def whole(out):
        return out.reshape(16, 32, 2, 8, 128).transpose(0, 1, 3, 2, 4).reshape(16, 16, 16, 256)

    return whole(value), whole(dens)


def solution(mesh):
    placed = (
        P("wind", None, "state", None),
        P("wind", None, "state", None),
        P("wind", None),
        P("wind", None),
        P(),
        P(),
    )
    return jax.shard_map(
        on_device,
        mesh=mesh,
        in_specs=placed,
        out_specs=(P("wind", None, "state", None), P("wind", None, "state", None)),
        check_vma=False,
    )
```

```python
import jax
import jax.numpy as jnp
from jax import lax
from jax.experimental import pallas as pl
from jax.experimental.pallas import tpu as pltpu
from jax.sharding import PartitionSpec as P

ITERS = 4
MESH = pl.DeviceIdType.MESH

step_size = 0.25
tank_spread = 0.3

F32 = jnp.float32
BF16 = jnp.bfloat16


def split(x):
    hi = x.astype(BF16)
    lo = (x - hi.astype(F32)).astype(BF16)
    return hi, lo


def product(x, r):
    return (
        jnp.dot(x[:, pl.ds(0, 256)], r[pl.ds(0, 256)], preferred_element_type=F32)
        + jnp.dot(x[:, pl.ds(256, 256)], r[pl.ds(0, 256)], preferred_element_type=F32)
        + jnp.dot(x[:, pl.ds(0, 256)], r[pl.ds(256, 256)], preferred_element_type=F32)
    )


def density_part(g, h, x, rs, d, pc, rb, still_ref, out_ref):
    point = lax.broadcasted_iota(jnp.int32, (128, 256), 1)
    winds = pl.ds(h * 8, 8)

    @pl.loop(0, 2)
    def _(c):
        @pl.loop(0, 4, unroll=4)
        def _(j):
            r = c * 4 + j
            rows = pl.ds(pl.multiple_of((g * 8 + r) * 16, 16), 16)
            tiles = pl.ds((g * 8 + r) * 2, 2)
            above = rb[g, h, pl.ds(r + 16, 256, stride=8), :]
            below = rb[g, h, pl.ds(r, 256, stride=8), :]
            drift = (-2.0 * jnp.tanh(0.25 * (above - below) + pc[g, h, pl.ds(r, 1), :])).T
            flux = drift * d[pl.ds(1 + h * 8, 8), rows, :].reshape(128, 256)
            upper = jnp.where(point == 255, 0.0, pltpu.roll(flux, 255, 1))
            lower = jnp.where(point == 0, 0.0, pltpu.roll(flux, 1, 1))
            still = jnp.concatenate(
                [still_ref[winds, tiles, kh].reshape(128, 128) for kh in range(2)], axis=1
            )
            hi, lo = split(still - (0.5 * step_size) * (upper - lower))
            at = pl.ds(pl.multiple_of(j * 128, 128), 128)
            x[at, pl.ds(0, 256)] = hi
            x[at, pl.ds(256, 256)] = lo

        out = product(x, rs)
        for j in range(4):
            for kh in range(2):
                out_ref[:, pl.ds((c * 4 + j) * 2, 2), kh] = out[
                    j * 128 : (j + 1) * 128, kh * 128 : (kh + 1) * 128
                ].reshape(8, 2, 8, 128)


def body(
    price_hbm,
    rate_hbm,
    tinv_hbm,
    sinv_hbm,
    v_hbm,
    d_hbm,
    vo,
    do,
    rs,
    d,
    pc,
    rb,
    u,
    uf,
    x,
    rt,
    pb,
    qb,
    dks,
    dkr,
    sb,
    price_s,
    rate_s,
    inv,
    held,
    held_d,
    ld_sem,
    hs,
    hr,
    ss,
    sr,
    dhs,
    dhr,
    dss,
    dsr,
    as_sem,
    ar_sem,
    own_sem,
    rl,
    fs,
):
    wi = lax.axis_index("wind")
    si = lax.axis_index("state")
    nw = 8
    ns = 16

    halves = (pl.ds(0, 128), pl.ds(128, 128))
    load_v = pltpu.make_async_copy(v_hbm, vo, ld_sem.at[0])
    load_d = pltpu.make_async_copy(d_hbm, d.at[pl.ds(1, 16)], ld_sem.at[1])
    load_v.start()
    load_d.start()
    small = [
        pltpu.make_async_copy(src, dst, ld_sem.at[2 + i])
        for i, (src, dst) in enumerate(
            ((price_hbm, price_s), (rate_hbm, rate_s), (tinv_hbm, inv.at[0]), (sinv_hbm, inv.at[1]))
        )
    ]
    for load in small:
        load.start()

    barrier = pltpu.get_barrier_semaphore()

    @pl.loop(1, ns)
    def _(p):
        pl.semaphore_signal(
            barrier, inc=1, device_id={"wind": wi, "state": (si + p) % ns}, device_id_type=MESH
        )

    @pl.when(wi > 0)
    def _():
        pl.semaphore_signal(barrier, inc=1, device_id={"wind": wi - 1, "state": si}, device_id_type=MESH)

    @pl.when(wi < nw - 1)
    def _():
        pl.semaphore_signal(barrier, inc=1, device_id={"wind": wi + 1, "state": si}, device_id_type=MESH)

    @pl.when(wi == 0)
    def _():
        d[0] = jnp.zeros((256, 256), F32)

        @pl.loop(0, ITERS)
        def _(n):
            for g in range(2):
                u[n, g, 0] = jnp.zeros((18, 8, 256), F32)

    @pl.when(wi == nw - 1)
    def _():
        d[17] = jnp.zeros((256, 256), F32)

        @pl.loop(0, ITERS)
        def _(n):
            for g in range(2):
                u[n, g, 17] = jnp.zeros((18, 8, 256), F32)

    @pl.when(si == 0)
    def _():
        dkr[0] = jnp.zeros((16, 16, 256), F32)

        @pl.loop(0, ITERS)
        def _(n):
            for g in range(2):
                u[n, g, pl.ds(1, 16), 0] = jnp.zeros((16, 8, 256), F32)

    @pl.when(si == ns - 1)
    def _():
        dkr[1] = jnp.zeros((16, 16, 256), F32)

        @pl.loop(0, ITERS)
        def _(n):
            for g in range(2):
                u[n, g, pl.ds(1, 16), 17] = jnp.zeros((16, 8, 256), F32)

    @pl.when(wi >= 2)
    def _():
        pl.semaphore_signal(barrier, inc=1, device_id={"wind": wi - 2, "state": si}, device_id_type=MESH)

    @pl.when(wi < nw - 2)
    def _():
        pl.semaphore_signal(barrier, inc=1, device_id={"wind": wi + 2, "state": si}, device_id_type=MESH)

    expected = ns - 1
    for near in (wi > 0, wi < nw - 1, wi >= 2, wi < nw - 2):
        expected = expected + jnp.where(near, 1, 0)
    pl.semaphore_wait(barrier, expected)

    def wind_part(n, g, up, k):
        points = pl.ds(1 + 4 * k, 4)
        return pltpu.make_async_remote_copy(
            src_ref=u.at[n, g, 16 if up else 1, points],
            dst_ref=u.at[n, g, 0 if up else 17, points],
            send_sem=hs.at[n, g, up, k],
            recv_sem=hr.at[n, g, up, k],
            device_id={"wind": wi + 1 if up else wi - 1, "state": si},
            device_id_type=MESH,
        )

    def wind_relay(n, g, up, k):
        return pltpu.make_async_remote_copy(
            src_ref=u.at[n, g, 16 if up else 1, pl.ds(1 + 4 * k, 4)],
            dst_ref=held.at[2 * n + g, k - 1],
            send_sem=hs.at[n, g, up, k],
            recv_sem=rl.at[2 * n + g, k - 1],
            device_id={"wind": wi + 2 if up else wi - 2, "state": si},
            device_id_type=MESH,
        )

    def wind_forward(n, g, up, k):
        return pltpu.make_async_remote_copy(
            src_ref=held.at[2 * n + g, k - 1],
            dst_ref=u.at[n, g, 0 if up else 17, pl.ds(1 + 4 * k, 4)],
            send_sem=fs.at[2 * n + g, k - 1],
            recv_sem=hr.at[n, g, up, k],
            device_id={"wind": wi - 1 if up else wi + 1, "state": si},
            device_id_type=MESH,
        )

    def dens_part(up, k):
        rows = pl.ds(64 * k, 64)
        return pltpu.make_async_remote_copy(
            src_ref=d_hbm.at[15 if up else 0, rows],
            dst_ref=d.at[0 if up else 17, rows],
            send_sem=dhs.at[up, k],
            recv_sem=dhr.at[up, k],
            device_id={"wind": wi + 1 if up else wi - 1, "state": si},
            device_id_type=MESH,
        )

    def dens_relay(up, k):
        return pltpu.make_async_remote_copy(
            src_ref=d_hbm.at[15 if up else 0, pl.ds(64 * k, 64)],
            dst_ref=held_d.at[k - 1],
            send_sem=dhs.at[up, k],
            recv_sem=rl.at[2 * ITERS, k - 1],
            device_id={"wind": wi + 2 if up else wi - 2, "state": si},
            device_id_type=MESH,
        )

    def dens_forward(up, k):
        return pltpu.make_async_remote_copy(
            src_ref=held_d.at[k - 1],
            dst_ref=d.at[0 if up else 17, pl.ds(64 * k, 64)],
            send_sem=fs.at[2 * ITERS, k - 1],
            recv_sem=dhr.at[up, k],
            device_id={"wind": wi - 1 if up else wi + 1, "state": si},
            device_id_type=MESH,
        )

    def both_hold(one, other):
        return jnp.logical_and(one, other)

    def has(up):
        return wi < nw - 1 if up else wi > 0

    def by_relay(up, k):
        if up:
            return both_hold(wi % 2 == 1, both_hold(wi >= 7 - 2 * k, wi <= 5))
        return both_hold(wi % 2 == 0, both_hold(wi >= 2, wi <= 2 * k))

    def relays(up, k):
        if up:
            return both_hold(wi % 2 == 1, wi >= 9 - 2 * k)
        return both_hold(wi % 2 == 0, wi <= 2 * k - 2)

    def start_plane(part, relay, up):
        @pl.when(has(up))
        def _():
            part(up, 0).start()

        for k in (1, 2, 3):

            @pl.when(by_relay(up, k))
            def _():
                relay(up, k).start()

            @pl.when(both_hold(has(up), jnp.logical_not(by_relay(up, k))))
            def _():
                part(up, k).start()

    def start_wind(n, g, up):
        start_plane(lambda up, k: wind_part(n, g, up, k), lambda up, k: wind_relay(n, g, up, k), up)

    def start_dens(up):
        start_plane(dens_part, dens_relay, up)

    def arrive_plane(part):
        for up in (0, 1):

            @pl.when(has(1 - up))
            def _():
                for k in range(4):
                    part(up, k).wait_recv()

    def drain_plane(part, onward):
        for up in (0, 1):

            @pl.when(has(up))
            def _():
                for k in range(4):
                    part(up, k).wait_send()

            for k in (1, 2, 3):

                @pl.when(relays(up, k))
                def _():
                    onward(up, k).wait_send()

    def pass_on(relay, onward):
        for k in (1, 2, 3):
            for up in (0, 1):

                @pl.when(relays(up, k))
                def _():
                    relay(up, k).wait_recv()
                    onward(up, k).start()

    def forward(n, g):
        pass_on(lambda up, k: wind_relay(n, g, up, k), lambda up, k: wind_forward(n, g, up, k))

    def forward_dens():
        pass_on(dens_relay, dens_forward)

    def state_copies(n, g):
        down = pltpu.make_async_remote_copy(
            src_ref=u.at[n, g, pl.ds(1, 16), 1],
            dst_ref=u.at[n, g, pl.ds(1, 16), 17],
            send_sem=ss.at[n, g, 0],
            recv_sem=sr.at[n, g, 0],
            device_id={"wind": wi, "state": si - 1},
            device_id_type=MESH,
        )
        up = pltpu.make_async_remote_copy(
            src_ref=u.at[n, g, pl.ds(1, 16), 16],
            dst_ref=u.at[n, g, pl.ds(1, 16), 0],
            send_sem=ss.at[n, g, 1],
            recv_sem=sr.at[n, g, 1],
            device_id={"wind": wi, "state": si + 1},
            device_id_type=MESH,
        )
        return down, up

    def dens_state_copies():
        down = pltpu.make_async_remote_copy(
            src_ref=dks.at[0],
            dst_ref=dkr.at[1],
            send_sem=dss.at[0],
            recv_sem=dsr.at[0],
            device_id={"wind": wi, "state": si - 1},
            device_id_type=MESH,
        )
        up = pltpu.make_async_remote_copy(
            src_ref=dks.at[1],
            dst_ref=dkr.at[0],
            send_sem=dss.at[1],
            recv_sem=dsr.at[1],
            device_id={"wind": wi, "state": si + 1},
            device_id_type=MESH,
        )
        return down, up

    def start(pair, index, last):
        @pl.when(index > 0)
        def _():
            pair[0].start()

        @pl.when(index < last)
        def _():
            pair[1].start()

    def arrive(pair, index, last):
        @pl.when(index < last)
        def _():
            pair[0].wait_recv()

        @pl.when(index > 0)
        def _():
            pair[1].wait_recv()

    def drain(pair, index, last):
        @pl.when(index > 0)
        def _():
            pair[0].wait_send()

        @pl.when(index < last)
        def _():
            pair[1].wait_send()

    start_dens(0)
    start_dens(1)

    def tile_rows(g, s, kh):
        return pl.ds(g * 256 + (s // 8) * 16 + kh * 8 + s % 8, 8, stride=32)

    load_v.wait()
    for g in range(2):

        @pl.loop(0, 16)
        def _(w):
            for s in range(16):
                for kh in range(2):
                    u[0, g, w + 1, s + 1, :, halves[kh]] = vo[w, tile_rows(g, s, kh), :]

        start_wind(0, g, 0)
        start_wind(0, g, 1)
        start(state_copies(0, g), si, ns - 1)

    load_d.wait()

    @pl.loop(0, 16)
    def _(w):
        for r in range(16):
            dks[0, w, pl.ds(r, 1), :] = d[w + 1, pl.ds(r * 16, 1), :]
            dks[1, w, pl.ds(r, 1), :] = d[w + 1, pl.ds(r * 16 + 15, 1), :]

    for load in small:
        load.wait()
    row = lax.broadcasted_iota(jnp.int32, (8, 128), 0)

    @pl.loop(0, 16)
    def _(w):
        for g in range(2):
            p = jnp.zeros((8, 128), F32)
            q = jnp.zeros((8, 128), F32)
            for r in range(8):
                p = jnp.where(row == r, price_s[w, g * 8 + r], p)
                q = jnp.where(row == r, rate_s[w, g * 8 + r], q)
            pb[g, w] = 0.5 * p
            qb[g, w] = step_size * q

    group = lax.broadcasted_iota(jnp.int32, (8, 128), 1) // 16
    for g in range(2):
        for h in range(2):
            rb[g, h, pl.ds(0, 8), :] = jnp.zeros((8, 128), F32)
            rb[g, h, pl.ds(2056, 8), :] = jnp.zeros((8, 128), F32)

            @pl.loop(0, 8)
            def _(r):
                p = jnp.zeros((1, 128), F32)
                for w in range(8):
                    p = jnp.where(group[:1] == w, 0.5 * price_s[h * 8 + w, g * 8 + r], p)
                pc[g, h, pl.ds(r, 1), :] = p

    for i, out in enumerate((rt, rs)):
        hi, lo = split(inv[i].T)
        out[pl.ds(0, 256)] = hi
        out[pl.ds(256, 256)] = lo

    def both(tile):
        return jnp.concatenate([tile, tile], axis=1)[None]

    def own_copy(g, h):
        return pltpu.make_async_copy(
            sb.at[g, h, si], rb.at[g, h, pl.ds(pl.multiple_of(8 + si * 128, 8), 128)], own_sem.at[g, h]
        )

    def regroup(g, h):
        @pl.loop(0, 4)
        def _(quad):
            for i in range(4):
                s = quad * 4 + i
                for kh in range(2):
                    a = [uf[g, h * 8 + w, s, :, halves[kh]] for w in range(8)]
                    for bit in (4, 2, 1):
                        high = (group // bit) % 2 == 1
                        b = [None] * 8
                        for w in range(8):
                            if w & bit == 0:
                                b[w] = jnp.where(high, pltpu.roll(a[w + bit], 16 * bit, 1), a[w])
                                b[w + bit] = jnp.where(high, a[w + bit], pltpu.roll(a[w], 128 - 16 * bit, 1))
                        a = b
                    for w in range(8):
                        sb[g, h, kh * 8 + w, pl.ds(pl.multiple_of(s * 8, 8), 8), :] = a[w]

    def send(g, h):
        own_copy(g, h).start()

        @pl.loop(1, ns)
        def _(p):
            q = (3 * p) % ns
            to = (si // 4 + q // 4) % 4 * 4 + (si // 2 + q // 2) % 2 * 2 + (si + q) % 2
            pltpu.make_async_remote_copy(
                src_ref=sb.at[g, h, to],
                dst_ref=rb.at[g, h, pl.ds(pl.multiple_of(8 + si * 128, 8), 128)],
                send_sem=as_sem.at[g, h],
                recv_sem=ar_sem.at[g, h],
                device_id={"wind": wi, "state": to},
                device_id_type=MESH,
            ).start()

    forward(0, 0)

    @pl.loop(0, 2 * ITERS)
    def _(m):
        n = m // 2
        g = m % 2
        arrive_plane(lambda up, k: wind_part(n, g, up, k))
        arrive(state_copies(n, g), si, ns - 1)

        @pl.when(m < 2 * ITERS - 1)
        def _():
            forward((m + 1) // 2, (m + 1) % 2)

        @pl.when(m == 1)
        def _():
            forward_dens()

        @pl.when(m == 2 * ITERS - 1)
        def _():
            for h in range(2):
                send(0, h)


        @pl.loop(0, 4)
        def _(turn):
            c = (turn * 3) % 4

            @pl.loop(0, 4)
            def _(j):
                w = c * 4 + j
                half = 0.25 * (u[n, g, w + 1, pl.ds(2, 16)] - u[n, g, w + 1, pl.ds(0, 16)]) + both(pb[g, w])
                t = jnp.tanh(half)
                mid = u[n, g, w + 1, pl.ds(1, 16)]
                couple = u[n, g, w + 2, pl.ds(1, 16)] + u[n, g, w, pl.ds(1, 16)] - 2.0 * mid
                source = (
                    u[0, g, w + 1, pl.ds(1, 16)] + 0.5 * t * (t - 2.0 * half) + both(qb[g, w]) * couple
                )
                hi, lo = split(source.reshape(128, 256))
                rows = pl.ds(pl.multiple_of(j * 128, 128), 128)
                x[rows, pl.ds(0, 256)] = hi
                x[rows, pl.ds(256, 256)] = lo

            swept = product(x, rt).reshape(4, 16, 8, 256)

            @pl.when(n < ITERS - 1)
            def _():
                u[n + 1, g, pl.ds(c * 4 + 1, 4), pl.ds(1, 16)] = swept

                @pl.when(turn == 0)
                def _():
                    start_wind(n + 1, g, 0)

                @pl.when(turn == 1)
                def _():
                    start_wind(n + 1, g, 1)

            @pl.when(n == ITERS - 1)
            def _():
                uf[g, pl.ds(c * 4, 4)] = swept

        @pl.when(n < ITERS - 1)
        def _():
            start(state_copies(n + 1, g), si, ns - 1)

        @pl.when(m == 0)
        def _():
            start(dens_state_copies(), si, ns - 1)

        @pl.when(n == ITERS - 1)
        def _():
            for h in range(2):
                regroup(g, h)

            @pl.when(g == 1)
            def _():
                for h in range(2):
                    send(1, h)

    @pl.loop(0, 16)
    def _(w):
        for g in range(2):
            for s in range(16):
                for kh in range(2):
                    vo[w, tile_rows(g, s, kh), :] = uf[g, w, s, :, halves[kh]]

    arrive_plane(dens_part)
    arrive(dens_state_copies(), si, ns - 1)
    level = lax.broadcasted_iota(jnp.int32, (16, 256), 0)

    @pl.loop(0, 16)
    def _(w):
        @pl.loop(0, 16)
        def _(r):
            rows = pl.ds(pl.multiple_of(r * 16, 16), 16)
            mid = d[w + 1, rows, :]
            above = jnp.where(level == 15, dkr[1, w, pl.ds(r, 1), :], pltpu.roll(mid, 15, 0))
            below = jnp.where(level == 0, dkr[0, w, pl.ds(r, 1), :], pltpu.roll(mid, 1, 0))
            couple = d[w + 2, rows, :] + d[w, rows, :] - 2.0 * mid
            source = (
                mid
                + (step_size * tank_spread) * (above + below - 2.0 * mid)
                + (step_size * rate_s[w, r]) * couple
            )
            for kh in range(2):
                do[w, pl.ds(r * 2, 2), kh] = source[:, kh * 128 : (kh + 1) * 128].reshape(2, 8, 128)

    def all_blocks(g, h, sem):
        blocks = sb.at[g, h, pl.ds(0, ns - 1)]
        return pltpu.make_async_copy(blocks, blocks, sem.at[g, h])

    @pl.loop(0, 4)
    def _(m):
        g = m // 2
        h = m % 2
        own_copy(g, h).wait()
        all_blocks(g, h, ar_sem).wait()

        @pl.when(m < 3)
        def _():
            density_part(g, h, x, rs, d, pc, rb, do, do.at[pl.ds(h * 8, 8), pl.ds(g * 16, 16)])

    @pl.loop(0, 4)
    def _(m):
        g = m // 2
        h = m % 2
        all_blocks(g, h, as_sem).wait()

    @pl.loop(0, 2 * ITERS)
    def _(m):
        n = m // 2
        g = m % 2
        drain_plane(lambda up, k: wind_part(n, g, up, k), lambda up, k: wind_forward(n, g, up, k))
        drain(state_copies(n, g), si, ns - 1)

    drain_plane(dens_part, dens_forward)
    drain(dens_state_copies(), si, ns - 1)


def finish(value_ref, still_ref, rs, d, pc, rb, value_hbm, dens_hbm, x, last, sem):
    copies = [
        pltpu.make_async_copy(value_ref.at[pl.ds(i * 4, 4)], value_hbm.at[pl.ds(i * 4, 4)], sem.at[i])
        for i in range(4)
    ]
    for i, (winds, tiles) in enumerate(
        ((pl.ds(0, 8), pl.ds(0, 16)), (pl.ds(8, 8), pl.ds(0, 16)), (pl.ds(0, 8), pl.ds(16, 16)))
    ):
        copies.append(
            pltpu.make_async_copy(still_ref.at[winds, tiles], dens_hbm.at[winds, tiles], sem.at[4 + i])
        )
    for copy in copies:
        copy.start()
    density_part(1, 1, x, rs, d, pc, rb, still_ref, last)
    ending = pltpu.make_async_copy(last, dens_hbm.at[pl.ds(8, 8), pl.ds(16, 16)], sem.at[7])
    ending.start()
    for copy in copies:
        copy.wait()
    ending.wait()


def on_device(value_next, density, price, wind_rate, tank_inverse, soc_inverse):
    vmem = pl.BlockSpec(memory_space=pltpu.VMEM)
    hbm = pl.BlockSpec(memory_space=pltpu.HBM)
    dma = pltpu.SemaphoreType.DMA
    tiles = value_next.reshape(16, 32, 8, 2, 128).transpose(0, 1, 3, 2, 4).reshape(16, 512, 128)
    value, dens, *rest = pl.pallas_call(
        body,
        name="storage_step",
        out_shape=(
            jax.ShapeDtypeStruct((16, 512, 128), F32),
            jax.ShapeDtypeStruct((16, 32, 2, 8, 128), F32),
            jax.ShapeDtypeStruct((512, 256), BF16),
            jax.ShapeDtypeStruct((18, 256, 256), F32),
            jax.ShapeDtypeStruct((2, 2, 8, 128), F32),
            jax.ShapeDtypeStruct((2, 2, 2064, 128), F32),
        ),
        in_specs=[hbm] * 6,
        out_specs=(vmem,) * 6,
        scratch_shapes=[
            pltpu.VMEM((ITERS, 2, 18, 18, 8, 256), F32),
            pltpu.VMEM((2, 16, 16, 8, 256), F32),
            pltpu.VMEM((512, 512), BF16),
            pltpu.VMEM((512, 256), BF16),
            pltpu.VMEM((2, 16, 8, 128), F32),
            pltpu.VMEM((2, 16, 8, 128), F32),
            pltpu.VMEM((2, 16, 16, 256), F32),
            pltpu.VMEM((2, 16, 16, 256), F32),
            pltpu.VMEM((2, 2, 16, 128, 128), F32),
            pltpu.SMEM((16, 16), F32),
            pltpu.SMEM((16, 16), F32),
            pltpu.VMEM((2, 256, 256), F32),
            pltpu.VMEM((2 * ITERS, 3, 4, 8, 256), F32),
            pltpu.VMEM((3, 64, 256), F32),
            dma((6,)),
            dma((ITERS, 2, 2, 4)),
            dma((ITERS, 2, 2, 4)),
            dma((ITERS, 2, 2)),
            dma((ITERS, 2, 2)),
            dma((2, 4)),
            dma((2, 4)),
            dma((2,)),
            dma((2,)),
            dma((2, 2)),
            dma((2, 2)),
            dma((2, 2)),
            dma((2 * ITERS + 1, 3)),
            dma((2 * ITERS + 1, 3)),
        ],
        compiler_params=pltpu.CompilerParams(
            collective_id=0, has_side_effects=True, vmem_limit_bytes=33 * 1024 * 1024
        ),
    )(*[pltpu.with_memory_space_constraint(a, pltpu.HBM) for a in (price, wind_rate, tank_inverse, soc_inverse, tiles, density.reshape(16, 256, 256))])

    value, dens = pl.pallas_call(
        finish,
        name="finish",
        out_shape=(
            jax.ShapeDtypeStruct((16, 512, 128), F32),
            jax.ShapeDtypeStruct((16, 32, 2, 8, 128), F32),
        ),
        in_specs=[vmem] * 6,
        out_specs=(hbm, hbm),
        scratch_shapes=[pltpu.VMEM((512, 512), BF16), pltpu.VMEM((8, 16, 2, 8, 128), F32), dma((8,))],
        compiler_params=pltpu.CompilerParams(vmem_limit_bytes=8 * 1024 * 1024),
    )(value, dens, *rest)

    def whole(out):
        return out.reshape(16, 32, 2, 8, 128).transpose(0, 1, 3, 2, 4).reshape(16, 16, 16, 256)

    return whole(value), whole(dens)


def solution(mesh):
    placed = (
        P("wind", None, "state", None),
        P("wind", None, "state", None),
        P("wind", None),
        P("wind", None),
        P(),
        P(),
    )
    return jax.shard_map(
        on_device,
        mesh=mesh,
        in_specs=placed,
        out_specs=(P("wind", None, "state", None), P("wind", None, "state", None)),
        check_vma=False,
    )
```
